256 devices in a mesh: seq: 8 (over z), ch: 32 (over x, y, core).
Axes of the slice: x: 4, y: 4, z: 8, core: 2. Of those that a mesh axis runs over, the one named last changes fastest.
Arguments:
- proj: bfloat16 [4, 2048, 3, 8192], P(None, ('seq', 'ch')), may hold values from -6 to 6
- short_w: float32 [3, 3, 8192], P(None, None, 'ch'), may hold values from -3.5 to 3.5
- long_filter: bfloat16 [512, 2048], P('ch'), may hold values from -1 to 1
Outputs:
- hyena_out: bfloat16 [4, 2048, 8192], P(None, ('seq', 'ch'))
The draws below stay inside these ranges and needn't reach their ends.
All inputs are finite; a program needn't handle non-finite values.
Results may differ from the reference program's by a relative error of at most 0.0085.
Values may be sent and summed in bfloat16 or wider, within the bound.
A program may use at most 128 MiB of HBM per device.

```python
import math
import jax
import jax.numpy as jnp
from jax import lax

D = 8192
GSIZE = 16
KS = 3
SEQS = 4
L = 2048
GROUPS = 512


def draw_long_filter(key, part):
    rate_key, noise_key = jax.random.split(jax.random.fold_in(key, 17))
    spread = jax.random.uniform(rate_key, (GROUPS, 1), jnp.float32)
    slowest = jnp.log(0.02 / L)
    fastest = jnp.log(1.0 / 40.0)
    noise = jax.random.truncated_normal(noise_key, -4.0, 4.0, (GROUPS, L), jnp.float32)
    decay = jnp.exp(slowest + spread * (fastest - slowest))
    positions = jnp.arange(L, dtype=jnp.float32)[None, :]
    normalizer = jnp.sqrt((1.0 - jnp.exp(-2.0 * decay)) / (1.0 - jnp.exp(-2.0 * decay * L)))
    return (noise * jnp.exp(-decay * positions) * normalizer).astype(jnp.bfloat16)


def block_levels(own_key, shape, cuts, low, high):
    gain, own = 1.0, jax.random.fold_in(own_key, 6)
    for dim, parts in cuts:
        draws = jnp.exp(jax.random.uniform(jax.random.fold_in(own, dim), (parts,), jnp.float32, low / len(cuts), high / len(cuts)))
        gain = gain * jnp.repeat(draws, shape[dim] // parts).reshape([-1 if axis == dim else 1 for axis in range(len(shape))])
    return gain


def normal_values(key, shape, deviation, bound, cuts=(), kind=jnp.bfloat16):
    result = jax.random.normal(key, shape, jnp.float32) * deviation
    if len(cuts) > 0:
        result = block_levels(key, shape, cuts, -0.22, 0.18) * result
    return jnp.clip(result, min=-bound, max=bound).astype(kind)


def setup_inputs(seed: int = 0) -> dict:
    seeds = jax.random.split(jax.random.key(seed), 4)
    return {
        "proj": normal_values(seeds[0], (SEQS, L, 3, D), 1.0, 6.0, ((1, 256),)),
        "short_w": normal_values(seeds[1], (KS, 3, D), KS ** -0.5, 3.5, ((2, 32),), jnp.float32),
        "long_filter": draw_long_filter(jax.random.fold_in(seeds[3], 71), 0),
    }


def reference(proj, short_w, long_filter):
    chan_block = math.gcd(D, 512)
    block_count = D // chan_block

    def one_block(block_index):
        first_chan = block_index * chan_block
        source = lax.dynamic_slice_in_dim(proj, first_chan, chan_block, 3).astype(jnp.float32)
        weights = lax.dynamic_slice_in_dim(short_w, first_chan, chan_block, 2).astype(jnp.float32)
        filter_taps = lax.dynamic_slice_in_dim(long_filter, first_chan // GSIZE, chan_block // GSIZE, 0).astype(jnp.float32)
        features = weights[0] * source
        for offset in range(1, KS):
            shifted = jnp.pad(source, ((0, 0), (offset, 0), (0, 0), (0, 0)))[:, :L]
            features = features + weights[offset] * shifted
        queries = features[:, :, 0].astype(jnp.bfloat16)
        product = (features[:, :, 1] * features[:, :, 2]).astype(jnp.bfloat16)
        kernel = jnp.repeat(filter_taps, GSIZE, axis=0).T
        spectrum = jnp.fft.rfft(product.astype(jnp.float32), n=2 * L, axis=1) * jnp.fft.rfft(kernel, n=2 * L, axis=0)[None]
        filtered = jnp.fft.irfft(spectrum, n=2 * L, axis=1)[:, :L]
        return (queries.astype(jnp.float32) * filtered).astype(jnp.bfloat16)

    blocks = lax.map(one_block, jnp.arange(block_count, dtype=jnp.int32))
    return jnp.moveaxis(blocks, 0, 2).reshape(SEQS, L, D)
```

```python
import jax
import jax.numpy as jnp
from jax import lax
from jax.experimental import pallas as pl
from jax.experimental.pallas import tpu as pltpu
from jax.sharding import PartitionSpec as P

MESH = pl.DeviceIdType.MESH
GSIZE = 16
LANES = 128
F32 = jnp.float32
BF16 = jnp.bfloat16


def kernel(nz, nc, proj, w_ref, lf_ref, out, kv, qb, qf, xs, xr, ys, yr, gs, toep, rev,
           kv_s, kv_r, q_s, q_r, h_s, h_r, x_s, x_r, y_s, y_r, o_s, o_r):
    z = lax.axis_index("seq")
    c = lax.axis_index("ch")
    seqs, _, rows, _ = proj.shape
    chans = kv.shape[-1]
    block = rows * nc
    halves = chans // LANES
    part = chans // nz
    per_half = LANES // part
    taps = w_ref.shape[0]
    chunk = 8
    chunks = nc // chunk
    span = chunk * rows

    def cols(p):
        return pl.ds(pl.multiple_of(p * chans, chans), chans)

    def settle(ref, sem):
        pltpu.make_async_copy(ref, ref, sem).wait()

    barrier = pltpu.get_barrier_semaphore()

    def greet_plane(k, carry):
        pl.semaphore_signal(barrier, inc=1, device_id=(z, lax.rem(c + k, nc)), device_id_type=MESH)
        return carry

    def greet_line(k, carry):
        pl.semaphore_signal(barrier, inc=1, device_id=(lax.rem(z + k, nz), c), device_id_type=MESH)
        return carry

    lax.fori_loop(1, nc, greet_plane, 0)
    lax.fori_loop(1, nz, greet_line, 0)
    own_kv = pltpu.make_async_copy(proj.at[:, 1:3, :, cols(c)], kv.at[c + 1], kv_r.at[c])
    own_kv.start()
    own_q = pltpu.make_async_copy(proj.at[:, 0, :, cols(c)], qb.at[c + 1], q_r.at[c])
    own_q.start()
    pl.semaphore_wait(barrier, nc - 1 + nz - 1)

    def send_kv(k, carry):
        p = lax.rem(c + k, nc)
        pltpu.make_async_remote_copy(
            src_ref=proj.at[:, 1:3, :, cols(p)], dst_ref=kv.at[c + 1], send_sem=kv_s,
            recv_sem=kv_r.at[c], device_id=(z, p), device_id_type=MESH).start()
        return carry

    def send_q(k, carry):
        p = lax.rem(c + k, nc)
        pltpu.make_async_remote_copy(
            src_ref=proj.at[:, 0, :, cols(p)], dst_ref=qb.at[c + 1], send_sem=q_s,
            recv_sem=q_r.at[c], device_id=(z, p), device_id_type=MESH).start()
        return carry

    lax.fori_loop(1, nc, send_kv, 0)
    lax.fori_loop(1, nc, send_q, 0)

    length = lf_ref.shape[1]
    pieces = length // LANES
    flip = (lax.broadcasted_iota(jnp.int32, (LANES, LANES), 0)
            + lax.broadcasted_iota(jnp.int32, (LANES, LANES), 1)) == LANES - 1
    flip = flip.astype(F32).astype(BF16)
    rev[:, 0:LANES] = jnp.zeros((lf_ref.shape[0], LANES), F32)
    for m in range(pieces):
        rev[:, (m + 1) * LANES:(m + 2) * LANES] = jnp.dot(
            lf_ref[:, m * LANES:(m + 1) * LANES], flip, preferred_element_type=F32)
    groups = part // GSIZE
    for g in range(groups):
        for m in range(pieces):
            pair = rev[pl.ds(z * groups + g, 1), m * LANES:(m + 2) * LANES]
            pair = jnp.broadcast_to(pair, (LANES, 2 * LANES))
            tile = pltpu.roll(pair, 1, 1, stride=1, stride_axis=0)[:, :LANES].astype(BF16)
            for th in range(2):
                for sh in range(2):
                    twice = m - th + sh
                    if twice % 2 == 0 and 0 <= twice // 2 < nz:
                        base = (twice // 2) * block + sh * LANES
                        toep[g, th * LANES:(th + 1) * LANES, base:base + LANES] = tile
        toep[g, 0:LANES, LANES:2 * LANES] = jnp.zeros((LANES, LANES), BF16)

    settle(kv.at[nc], kv_r.at[nc - 1])
    settle(qb.at[nc], q_r.at[nc - 1])

    @pl.when(z < nz - 1)
    def _():
        pltpu.make_async_remote_copy(
            src_ref=kv.at[nc], dst_ref=kv.at[0], send_sem=h_s.at[0], recv_sem=h_r.at[0],
            device_id=(z + 1, c), device_id_type=MESH).start()
        pltpu.make_async_remote_copy(
            src_ref=qb.at[nc], dst_ref=qb.at[0], send_sem=h_s.at[1], recv_sem=h_r.at[1],
            device_id=(z + 1, c), device_id_type=MESH).start()

    @pl.when(z == 0)
    def _():
        kv[0] = jnp.zeros(kv.shape[1:], BF16)
        qb[0] = jnp.zeros(qb.shape[1:], BF16)

    def feature(ext, i, h):
        total = None
        for k in range(taps):
            term = w_ref[k, i:i + 1, h * LANES:(h + 1) * LANES] * ext[rows - k:rows - k + span]
            total = term if total is None else total + term
        return total

    def product_chunk(k, carry):
        j = lax.rem(k + 1, chunks)
        s0 = j * chunk

        def arrive(s, carry):
            settle(kv.at[s + 1], kv_r.at[s])
            return carry

        first = s0 - (k == 0).astype(jnp.int32)
        last = s0 + chunk - (k >= chunks - 2).astype(jnp.int32)
        lax.fori_loop(first, last, arrive, 0)

        @pl.when(jnp.logical_and(j == 0, z > 0))
        def _():
            settle(kv.at[0], h_r.at[0])

        t0 = pl.multiple_of(j * span, span)
        for h in range(halves):
            prods = []
            for n in range(seqs):
                feats = []
                for i in range(2):
                    ext = kv[pl.ds(s0, chunk + 1), n, i, :, h * LANES:(h + 1) * LANES].astype(F32)
                    feats.append(feature(ext.reshape((chunk + 1) * rows, LANES), i + 1, h))
                prods.append(feats[0] * feats[1])
            for k in range(per_half):
                tile = jnp.concatenate([p[:, k * part:(k + 1) * part] for p in prods], axis=1)
                xs[h * per_half + k, pl.ds(t0, span), :] = tile.astype(BF16)
        return carry

    lax.fori_loop(0, chunks, product_chunk, 0)

    def send_x(k, carry):
        p = lax.rem(z + k, nz)
        pltpu.make_async_remote_copy(
            src_ref=xs.at[p], dst_ref=xr.at[nz - 1 - z], send_sem=x_s, recv_sem=x_r.at[z],
            device_id=(p, c), device_id_type=MESH).start()
        return carry

    lax.fori_loop(1, nz, send_x, 0)
    pltpu.make_async_copy(xs.at[z], xr.at[nz - 1 - z], x_r.at[z]).start()
    xr[nz] = jnp.zeros(xr.shape[1:], BF16)

    def query_chunk(k, carry):
        j = lax.rem(k + 1, chunks)
        s0 = j * chunk

        def arrive(s, carry):
            settle(qb.at[s + 1], q_r.at[s])
            return carry

        first = s0 - (k == 0).astype(jnp.int32)
        last = s0 + chunk - (k >= chunks - 2).astype(jnp.int32)
        lax.fori_loop(first, last, arrive, 0)

        @pl.when(jnp.logical_and(j == 0, z > 0))
        def _():
            settle(qb.at[0], h_r.at[1])

        for h in range(halves):
            for n in range(seqs):
                ext = qb[pl.ds(s0, chunk + 1), n, :, h * LANES:(h + 1) * LANES].astype(F32)
                value = feature(ext.reshape((chunk + 1) * rows, LANES), 0, h)
                qf[pl.ds(s0, chunk), n, :, h * LANES:(h + 1) * LANES] = value.astype(BF16).reshape(
                    chunk, rows, LANES)
        return carry

    lax.fori_loop(0, chunks, query_chunk, 0)

    for s in range(nz):
        settle(xr.at[nz - 1 - s], x_r.at[s])
    lane = lax.broadcasted_iota(jnp.int32, (1, 2 * LANES), 1)
    for m in range(nz // 2):
        lags = 2 * m + 2
        even = xr[nz - 1 - 2 * m:nz - 1 - 2 * m + lags].reshape(lags * block, LANES)
        odd = xr[nz - 2 - 2 * m:nz - 2 - 2 * m + lags].reshape(lags * block, LANES)
        both = jnp.concatenate([even, odd], axis=1)
        total = None
        for g in range(groups):
            keep = ((lane // GSIZE) % groups == g).astype(F32).astype(BF16)
            term = jnp.dot(toep[g, :, 0:lags * block], both * keep, preferred_element_type=F32)
            total = term if total is None else total + term
        ys[2 * m] = total[:, :LANES].astype(BF16)
        ys[2 * m + 1] = total[:, LANES:].astype(BF16)

    def send_y(k, carry):
        p = lax.rem(z + k, nz)
        pltpu.make_async_remote_copy(
            src_ref=ys.at[p], dst_ref=yr.at[z], send_sem=y_s, recv_sem=y_r.at[z],
            device_id=(p, c), device_id_type=MESH).start()
        return carry

    lax.fori_loop(1, nz, send_y, 0)
    pltpu.make_async_copy(ys.at[z], yr.at[z], y_r.at[z]).start()
    for s in range(nz):
        settle(yr.at[s], y_r.at[s])

    def gate_chunk(j, carry):
        s0 = j * chunk
        t0 = pl.multiple_of(j * span, span)
        for h in range(halves):
            tiles = [yr[h * per_half + k, pl.ds(t0, span), :].astype(F32) for k in range(per_half)]
            for n in range(seqs):
                filtered = jnp.concatenate([t[:, n * part:(n + 1) * part] for t in tiles], axis=1)
                query = qf[pl.ds(s0, chunk), n, :, h * LANES:(h + 1) * LANES].astype(F32)
                gated = query * filtered.reshape(chunk, rows, LANES)
                gs[pl.ds(s0, chunk), n, :, h * LANES:(h + 1) * LANES] = gated.astype(BF16)

        def send_out(s, carry):
            @pl.when(s != c)
            def _():
                pltpu.make_async_remote_copy(
                    src_ref=gs.at[s], dst_ref=out.at[:, :, cols(c)], send_sem=o_s, recv_sem=o_r.at[c],
                    device_id=(z, s), device_id_type=MESH).start()

            @pl.when(s == c)
            def _():
                pltpu.make_async_copy(gs.at[c], out.at[:, :, cols(c)], o_r.at[c]).start()
            return carry

        lax.fori_loop(s0, s0 + chunk, send_out, 0)
        return carry

    lax.fori_loop(0, chunks, gate_chunk, 0)

    def landed(s, carry):
        settle(out.at[:, :, cols(s)], o_r.at[s])
        return carry

    lax.fori_loop(0, nc, landed, 0)
    settle(kv.at[1:nc], kv_s)
    settle(qb.at[1:nc], q_s)
    settle(xs.at[1:nz], x_s)
    settle(ys.at[1:nz], y_s)
    settle(gs.at[1:nc], o_s)

    @pl.when(z < nz - 1)
    def _():
        settle(kv.at[nc], h_s.at[0])
        settle(qb.at[nc], h_s.at[1])


def solution(mesh):
    nz, nc = mesh.shape["seq"], mesh.shape["ch"]

    def shards(proj, short_w, long_filter):
        seqs, rows, _, width = proj.shape
        chans = width // nc
        block = rows * nc
        groups, length = long_filter.shape
        own = chans // nz // GSIZE
        by_component = jnp.transpose(proj, (0, 2, 1, 3))
        dma = pltpu.SemaphoreType.DMA
        return pl.pallas_call(
            lambda *refs: kernel(nz, nc, *refs),
            out_shape=jax.ShapeDtypeStruct((seqs, rows, width), BF16),
            in_specs=[
                pl.BlockSpec(memory_space=pl.ANY),
                pl.BlockSpec(memory_space=pltpu.VMEM),
                pl.BlockSpec(memory_space=pltpu.VMEM),
            ],
            out_specs=pl.BlockSpec(memory_space=pl.ANY),
            scratch_shapes=[
                pltpu.VMEM((nc + 1, seqs, 2, rows, chans), BF16),
                pltpu.VMEM((nc + 1, seqs, rows, chans), BF16),
                pltpu.VMEM((nc, seqs, rows, chans), BF16),
                pltpu.VMEM((nz, block, LANES), BF16),
                pltpu.VMEM((nz + 1, block, LANES), BF16),
                pltpu.VMEM((nz, block, LANES), BF16),
                pltpu.VMEM((nz, block, LANES), BF16),
                pltpu.VMEM((nc, seqs, rows, chans), BF16),
                pltpu.VMEM((own, block, length), BF16),
                pltpu.VMEM((groups, length + LANES), F32),
                dma, dma((nc,)), dma, dma((nc,)), dma((2,)), dma((2,)),
                dma, dma((nz,)), dma, dma((nz,)), dma, dma((nc,)),
            ],
            compiler_params=pltpu.CompilerParams(collective_id=0, has_side_effects=True),
            name="hyena",
        )(by_component, short_w, long_filter)

    in_specs = (P(None, ("seq", "ch"), None, None), P(None, None, "ch"), P("ch", None))
    out_specs = P(None, ("seq", "ch"), None)
    return jax.shard_map(shards, mesh=mesh, in_specs=in_specs, out_specs=out_specs, check_vma=False)
```

```python
import jax
import jax.numpy as jnp
from jax import lax
from jax.experimental import pallas as pl
from jax.experimental.pallas import tpu as pltpu
from jax.sharding import PartitionSpec as P

MESH = pl.DeviceIdType.MESH
GSIZE = 16
LANES = 128
F32 = jnp.float32
BF16 = jnp.bfloat16


def kernel(nz, nc, proj, w_ref, lf_ref, out, kv, qb, qf, xs, xr, ys, yr, gs, toep, rev,
           kv_s, kv_r, q_s, q_r, h_s, h_r, x_s, x_r, y_s, y_r, o_s, o_r):
    z = lax.axis_index("seq")
    c = lax.axis_index("ch")
    seqs, _, rows, _ = proj.shape
    halves, chans = kv.shape[0], qb.shape[-1]
    block = rows * nc
    part = chans // nz
    per_half = LANES // part
    taps = w_ref.shape[0]
    chunk = 8
    chunks = nc // chunk
    span = chunk * rows
    own_half = lax.rem(z, halves)
    side = 4
    around = (0, 2, 1, 3)

    def cols(p):
        return pl.ds(pl.multiple_of(p * chans, chans), chans)

    def half_cols(p, h):
        return pl.ds(pl.multiple_of(p * chans + h * LANES, LANES), LANES)

    def settle(ref, sem):
        pltpu.make_async_copy(ref, ref, sem).wait()

    def partner(k):
        x = lax.rem(c // 8 + 2 + k // 8, side)
        y = lax.rem(c // 2 + 2 + k // 2, side)
        return x * 8 + y * 2 + lax.rem(c + k, 2)

    def each_partner(body):
        def step(k, carry):
            body(partner(k))
            return carry

        lax.fori_loop(0, 20, step, 0)
        lax.fori_loop(21, nc, step, 0)

    barrier = pltpu.get_barrier_semaphore()

    def greet(p):
        pl.semaphore_signal(barrier, inc=1, device_id=(z, p), device_id_type=MESH)

    def greet_line(k, carry):
        pl.semaphore_signal(barrier, inc=1, device_id=(lax.rem(z + k, nz), c), device_id_type=MESH)
        return carry

    each_partner(greet)
    lax.fori_loop(1, nz, greet_line, 0)
    for h in range(halves):
        pltpu.make_async_copy(
            proj.at[:, 1:3, :, half_cols(c, h)], kv.at[h, c + 1], kv_r.at[h, c]).start()
    pltpu.make_async_copy(proj.at[:, 0, :, cols(c)], qb.at[c + 1], q_r).start()
    pl.semaphore_wait(barrier, nc - 1 + nz - 1)

    for h in range(halves):
        def send_kv(p, h=h):
            pltpu.make_async_remote_copy(
                src_ref=proj.at[:, 1:3, :, half_cols(p, h)], dst_ref=kv.at[h, c + 1], send_sem=kv_s,
                recv_sem=kv_r.at[h, c], device_id=(z, p), device_id_type=MESH).start()

        each_partner(send_kv)

    length = lf_ref.shape[1]
    pieces = length // LANES
    flip = (lax.broadcasted_iota(jnp.int32, (LANES, LANES), 0)
            + lax.broadcasted_iota(jnp.int32, (LANES, LANES), 1)) == LANES - 1
    flip = flip.astype(F32).astype(BF16)
    rev[:, 0:LANES] = jnp.zeros((lf_ref.shape[0], LANES), F32)
    for m in range(pieces):
        rev[:, (m + 1) * LANES:(m + 2) * LANES] = jnp.dot(
            lf_ref[:, m * LANES:(m + 1) * LANES], flip, preferred_element_type=F32)
    groups = part // GSIZE
    own_row = (own_half * LANES + (z // halves) * part) // GSIZE
    for g in range(groups):
        for m in range(pieces):
            pair = rev[pl.ds(own_row + g, 1), m * LANES:(m + 2) * LANES]
            pair = jnp.broadcast_to(pair, (LANES, 2 * LANES))
            tile = pltpu.roll(pair, 1, 1, stride=1, stride_axis=0)[:, :LANES].astype(BF16)
            for th in range(2):
                for sh in range(2):
                    twice = m - th + sh
                    if twice % 2 == 0 and 0 <= twice // 2 < nz:
                        base = (twice // 2) * block + sh * LANES
                        toep[g, th * LANES:(th + 1) * LANES, base:base + LANES] = tile
        toep[g, 0:LANES, LANES:2 * LANES] = jnp.zeros((LANES, LANES), BF16)

    xr[nz] = jnp.zeros(xr.shape[1:], BF16)

    @pl.when(z == 0)
    def _():
        for h in range(halves):
            kv[h, 0] = jnp.zeros(kv.shape[2:], BF16)
        qb[0] = jnp.zeros(qb.shape[1:], BF16)

    def feature(ext, i, h):
        total = None
        for k in range(taps):
            term = w_ref[k, i:i + 1, h * LANES:(h + 1) * LANES] * ext[rows - k:rows - k + span]
            total = term if total is None else total + term
        return total

    for h in range(halves):
        settle(kv.at[h, nc], kv_r.at[h, nc - 1])

        @pl.when(z < nz - 1)
        def _():
            pltpu.make_async_remote_copy(
                src_ref=kv.at[h, nc], dst_ref=kv.at[h, 0], send_sem=h_s.at[h], recv_sem=h_r.at[h],
                device_id=(z + 1, c), device_id_type=MESH).start()

        def product_chunk(k, carry, h=h):
            j = lax.rem(k + 1, chunks)
            s0 = j * chunk

            def arrive(s, carry):
                settle(kv.at[h, s + 1], kv_r.at[h, s])
                return carry

            first = s0 - (k == 0).astype(jnp.int32)
            last = s0 + chunk - (k >= chunks - 2).astype(jnp.int32)
            lax.fori_loop(first, last, arrive, 0)

            @pl.when(jnp.logical_and(j == 0, z > 0))
            def _():
                settle(kv.at[h, 0], h_r.at[h])

            t0 = pl.multiple_of(j * span, span)
            prods = []
            for n in range(seqs):
                feats = []
                for i in range(2):
                    ext = kv[h, pl.ds(s0, chunk + 1), n, i].astype(F32)
                    feats.append(feature(ext.reshape((chunk + 1) * rows, LANES), i + 1, h))
                prods.append(feats[0] * feats[1])
            for k in range(per_half):
                tile = jnp.concatenate([p[:, k * part:(k + 1) * part] for p in prods], axis=1)
                xs[halves * k + h, pl.ds(t0, span), :] = tile.astype(BF16)
            return carry

        lax.fori_loop(0, chunks, product_chunk, 0)

        for a in (2, 1, 3, 0):
            p = halves * lax.rem(z // halves + a, per_half) + h

            def send_x(p=p):
                pltpu.make_async_remote_copy(
                    src_ref=xs.at[p], dst_ref=xr.at[nz - 1 - z], send_sem=x_s, recv_sem=x_r.at[z],
                    device_id=(p, c), device_id_type=MESH).start()

            if a > 0:
                send_x()
            else:
                pl.when(own_half != h)(send_x)

        @pl.when(own_half == h)
        def _():
            pltpu.make_async_copy(xs.at[z], xr.at[nz - 1 - z], x_r.at[z]).start()

        if h == 0:
            def send_q(p):
                pltpu.make_async_remote_copy(
                    src_ref=proj.at[:, 0, :, cols(p)], dst_ref=qb.at[c + 1], send_sem=q_s,
                    recv_sem=q_r, device_id=(z, p), device_id_type=MESH).start()

            each_partner(send_q)

    settle(qb.at[1:nc + 1], q_r)

    @pl.when(z < nz - 1)
    def _():
        pltpu.make_async_remote_copy(
            src_ref=qb.at[nc], dst_ref=qb.at[0], send_sem=h_s.at[2], recv_sem=h_r.at[2],
            device_id=(z + 1, c), device_id_type=MESH).start()

    for s in range(nz):
        settle(xr.at[nz - 1 - s], x_r.at[s])
    lane = lax.broadcasted_iota(jnp.int32, (1, 2 * LANES), 1)
    for m in range(nz // 2):
        lags = 2 * m + 2
        even = xr[nz - 1 - 2 * m:nz - 1 - 2 * m + lags].reshape(lags * block, LANES)
        odd = xr[nz - 2 - 2 * m:nz - 2 - 2 * m + lags].reshape(lags * block, LANES)
        both = jnp.concatenate([even, odd], axis=1)
        total = None
        for g in range(groups):
            keep = ((lane // GSIZE) % groups == g).astype(F32).astype(BF16)
            term = jnp.dot(toep[g, :, 0:lags * block], both * keep, preferred_element_type=F32)
            total = term if total is None else total + term
        for i, values in enumerate((total[:, :LANES], total[:, LANES:])):
            ys[2 * m + i] = values.astype(BF16)
            p = 2 * m + i

            @pl.when(z != p)
            def _():
                pltpu.make_async_remote_copy(
                    src_ref=ys.at[p], dst_ref=yr.at[z], send_sem=y_s, recv_sem=y_r.at[z],
                    device_id=(p, c), device_id_type=MESH).start()

            @pl.when(z == p)
            def _():
                pltpu.make_async_copy(ys.at[p], yr.at[p], y_r.at[p]).start()

    @pl.when(z > 0)
    def _():
        settle(qb.at[0], h_r.at[2])

    def query_chunk(j, carry):
        s0 = j * chunk
        for h in range(halves):
            for n in range(seqs):
                ext = qb[pl.ds(s0, chunk + 1), n, :, h * LANES:(h + 1) * LANES].astype(F32)
                value = feature(ext.reshape((chunk + 1) * rows, LANES), 0, h)
                qf[pl.ds(s0, chunk), n, :, h * LANES:(h + 1) * LANES] = value.astype(BF16).reshape(
                    chunk, rows, LANES)
        return carry

    lax.fori_loop(0, chunks, query_chunk, 0)

    for h in range(halves):
        for k in range(per_half):
            settle(yr.at[halves * k + h], y_r.at[halves * k + h])

        def gate_chunk(j, carry, h=h):
            s0 = j * chunk
            t0 = pl.multiple_of(j * span, span)
            tiles = [yr[halves * k + h, pl.ds(t0, span), :].astype(F32) for k in range(per_half)]
            for n in range(seqs):
                filtered = jnp.concatenate([t[:, n * part:(n + 1) * part] for t in tiles], axis=1)
                query = qf[pl.ds(s0, chunk), n, :, h * LANES:(h + 1) * LANES].astype(F32)
                gated = query * filtered.reshape(chunk, rows, LANES)
                gs[h, pl.ds(s0, chunk), n] = gated.astype(BF16)
            return carry

        lax.fori_loop(0, chunks, gate_chunk, 0)

        def send_out(p, h=h):
            pltpu.make_async_remote_copy(
                src_ref=gs.at[h, p], dst_ref=out.at[:, :, half_cols(c, h)], send_sem=o_s, recv_sem=o_r,
                device_id=(z, p), device_id_type=MESH).start()

        each_partner(send_out)
        pltpu.make_async_copy(gs.at[h, c], out.at[:, :, half_cols(c, h)], o_r).start()

    settle(kv.at[:, 1:nc], kv_s)
    settle(qb.at[1:nc], q_s)
    settle(xs.at[1:nz], x_s)
    settle(ys.at[1:nz], y_s)

    @pl.when(z < nz - 1)
    def _():
        for h in range(halves):
            settle(kv.at[h, nc], h_s.at[h])
        settle(qb.at[nc], h_s.at[2])

    settle(gs.at[:, 1:nc], o_s)
    settle(out, o_r)


def solution(mesh):
    nz, nc = mesh.shape["seq"], mesh.shape["ch"]

    def shards(proj, short_w, long_filter):
        seqs, rows, _, width = proj.shape
        chans = width // nc
        block = rows * nc
        halves = chans // LANES
        groups, length = long_filter.shape
        own = chans // nz // GSIZE
        by_component = jnp.transpose(proj, (0, 2, 1, 3))
        dma = pltpu.SemaphoreType.DMA
        return pl.pallas_call(
            lambda *refs: kernel(nz, nc, *refs),
            out_shape=jax.ShapeDtypeStruct((seqs, rows, width), BF16),
            in_specs=[
                pl.BlockSpec(memory_space=pl.ANY),
                pl.BlockSpec(memory_space=pltpu.VMEM),
                pl.BlockSpec(memory_space=pltpu.VMEM),
            ],
            out_specs=pl.BlockSpec(memory_space=pl.ANY),
            scratch_shapes=[
                pltpu.VMEM((halves, nc + 1, seqs, 2, rows, LANES), BF16),
                pltpu.VMEM((nc + 1, seqs, rows, chans), BF16),
                pltpu.VMEM((nc, seqs, rows, chans), BF16),
                pltpu.VMEM((nz, block, LANES), BF16),
                pltpu.VMEM((nz + 1, block, LANES), BF16),
                pltpu.VMEM((nz, block, LANES), BF16),
                pltpu.VMEM((nz, block, LANES), BF16),
                pltpu.VMEM((halves, nc, seqs, rows, LANES), BF16),
                pltpu.VMEM((own, block, length), BF16),
                pltpu.VMEM((groups, length + LANES), F32),
                dma, dma((halves, nc)), dma, dma, dma((3,)), dma((3,)),
                dma, dma((nz,)), dma, dma((nz,)), dma, dma,
            ],
            compiler_params=pltpu.CompilerParams(collective_id=0, has_side_effects=True),
            name="hyena",
        )(by_component, short_w, long_filter)

    in_specs = (P(None, ("seq", "ch"), None, None), P(None, None, "ch"), P("ch", None))
    out_specs = P(None, ("seq", "ch"), None)
    return jax.shard_map(shards, mesh=mesh, in_specs=in_specs, out_specs=out_specs, check_vma=False)
```

```python
import jax
import jax.numpy as jnp
from jax import lax
from jax.experimental import pallas as pl
from jax.experimental.pallas import tpu as pltpu
from jax.sharding import PartitionSpec as P

MESH = pl.DeviceIdType.MESH
GSIZE = 16
LANES = 128
F32 = jnp.float32
BF16 = jnp.bfloat16


def kernel(nz, nc, proj_in, w_in, lf_in, out, proj, w_ref, lf_ref, kv, qb, qf, xs, xr, xu, wl, ys, yr, gs, toep, rev,
           in_r, kv_s, kv_r, q_s, q_r, h_s, h_r, x_s, x_r, y_s, y_r, o_s, o_r):
    z = lax.axis_index("seq")
    c = lax.axis_index("ch")
    seqs, _, rows, _ = proj.shape
    halves, pairs, chans = kv.shape[0], kv.shape[1], qb.shape[-1]
    duo = seqs // pairs
    block = rows * nc
    part = chans // nz
    per_half = LANES // part
    taps = w_ref.shape[0]
    chunk = 8
    chunks = nc // chunk
    span = chunk * rows
    folds = block // LANES
    fold_slots = nc // folds
    strips = fold_slots // chunk
    own_half = lax.rem(z, halves)
    side = 4
    around = (2, 1, 3, 0)
    line = (4, 3, 5, 2, 6, 1, 7)

    def cols(p):
        return pl.ds(pl.multiple_of(p * chans, chans), chans)

    def half_cols(p, h):
        return pl.ds(pl.multiple_of(p * chans + h * LANES, LANES), LANES)

    def settle(ref, sem):
        pltpu.make_async_copy(ref, ref, sem).wait()

    across = [lax.rem(c // 8 + d, side) * 8 for d in range(side)]
    along = [lax.rem(c // 2 + d, side) * 2 for d in range(side)]
    core = [lax.rem(c + d, 2) for d in range(2)]

    def each_partner(body):
        for dx in around:
            for dy in around:
                for dc in (1, 0):
                    if (dx, dy, dc) != (0, 0, 0):
                        body(across[dx] + along[dy] + core[dc])

    barrier = pltpu.get_barrier_semaphore()

    def greet(p):
        pl.semaphore_signal(barrier, inc=1, device_id=(z, p), device_id_type=MESH)

    for n in range(seqs):
        pltpu.make_async_copy(proj_in.at[n], proj.at[n], in_r.at[0]).start()
    pltpu.make_async_copy(lf_in, lf_ref, in_r.at[1]).start()
    pltpu.make_async_copy(w_in, w_ref, in_r.at[2]).start()
    each_partner(greet)
    for d in line:
        pl.semaphore_signal(barrier, inc=1, device_id=(lax.rem(z + d, nz), c), device_id_type=MESH)
    settle(proj, in_r.at[0])
    last = c // (nc - 1)
    for h in range(halves):
        for a in range(pairs):
            pltpu.make_async_copy(
                proj.at[a * duo:(a + 1) * duo, 1:3, :, half_cols(c, h)], kv.at[h, a, c + 1],
                kv_r.at[h, a]).start()
    pltpu.make_async_copy(proj.at[:, 0, :, cols(c)], qb.at[c + 1], q_r.at[last]).start()
    pl.semaphore_wait(barrier, nc - 1 + nz - 1)

    for h in range(halves):
        for a in range(pairs):
            def send_kv(p, h=h, a=a):
                pltpu.make_async_remote_copy(
                    src_ref=proj.at[a * duo:(a + 1) * duo, 1:3, :, half_cols(p, h)],
                    dst_ref=kv.at[h, a, c + 1], send_sem=kv_s, recv_sem=kv_r.at[h, a],
                    device_id=(z, p), device_id_type=MESH).start()

            each_partner(send_kv)

    settle(lf_ref, in_r.at[1])
    settle(w_ref, in_r.at[2])

    length = lf_ref.shape[1]
    pieces = length // LANES
    flip = (lax.broadcasted_iota(jnp.int32, (LANES, LANES), 0)
            + lax.broadcasted_iota(jnp.int32, (LANES, LANES), 1)) == LANES - 1
    flip = flip.astype(F32).astype(BF16)
    rev[:, 0:LANES] = jnp.zeros((lf_ref.shape[0], LANES), F32)
    for m in range(pieces):
        rev[:, (m + 1) * LANES:(m + 2) * LANES] = jnp.dot(
            lf_ref[:, m * LANES:(m + 1) * LANES], flip, preferred_element_type=F32)
    groups = part // GSIZE
    own_row = (own_half * LANES + (z // halves) * part) // GSIZE
    for g in range(groups):
        for m in range(pieces):
            pair = rev[pl.ds(own_row + g, 1), m * LANES:(m + 2) * LANES]
            pair = jnp.broadcast_to(pair, (LANES, 2 * LANES))
            tile = pltpu.roll(pair, 1, 1, stride=1, stride_axis=0)[:, :LANES]
            tile = tile.astype(BF16)
            for th in range(2):
                for sh in range(2):
                    twice = m - th + sh
                    if twice % 2 == 0 and 0 <= twice // 2 < nz:
                        base = (twice // 2) * block + sh * LANES
                        toep[g, th * LANES:(th + 1) * LANES, base:base + LANES] = tile
        toep[g, 0:LANES, LANES:2 * LANES] = jnp.zeros((LANES, LANES), BF16)

    for k in range(taps):
        for i in range(2):
            mine = jnp.where(own_half == 0, w_ref[k, i + 1:i + 2, :LANES], w_ref[k, i + 1:i + 2, LANES:])
            mine = pltpu.roll(jnp.broadcast_to(mine, (rows, LANES)), LANES - (z // halves) * part, 1)
            wl[k, i] = jnp.concatenate([mine[:, :part]] * seqs, axis=1)

    xu[nz] = jnp.zeros(xu.shape[1:], BF16)
    row = lax.broadcasted_iota(jnp.int32, (rows, LANES), 0)
    for h in range(halves):
        for a in range(pairs):
            kv[h, a, 0] = jnp.zeros(kv.shape[3:], BF16)

    @pl.when(z == 0)
    def _():
        qb[0] = jnp.zeros(qb.shape[1:], BF16)

    def feature(ext, i, h):
        total = None
        for k in range(taps):
            term = w_ref[k, i:i + 1, h * LANES:(h + 1) * LANES] * ext[rows - k:rows - k + span]
            total = term if total is None else total + term
        return total

    def send_q(p):
        pltpu.make_async_remote_copy(
            src_ref=proj.at[:, 0, :, cols(p)], dst_ref=qb.at[c + 1], send_sem=q_s,
            recv_sem=q_r.at[last], device_id=(z, p), device_id_type=MESH).start()

    for h in range(halves):
        for a in range(pairs):
            settle(kv.at[h, a, 1:nc + 1], kv_r.at[h, a])

            def product_strip(k, carry, h=h, a=a):
                j = strips - 1 - k

                prods = []
                for f in range(folds):
                    for n in range(duo):
                        feats = []
                        for i in range(2):
                            ext = kv[h, a, pl.ds(f * fold_slots + j * chunk, chunk + 1), n, i].astype(F32)
                            feats.append(feature(ext.reshape((chunk + 1) * rows, LANES), i + 1, h))
                        prods.append(feats[0] * feats[1])
                t0 = pl.multiple_of(j * span, span)
                for k in range(per_half):
                    tile = jnp.concatenate([p[:, k * part:(k + 1) * part] for p in prods], axis=1)
                    xs[halves * k + h, a, pl.ds(t0, span), :] = tile.astype(BF16)
                return carry

            lax.fori_loop(0, strips, product_strip, 0)

            rims = []
            for n in range(duo):
                rim = pltpu.roll(kv[h, a, 1, n, 1].astype(F32), 6, 0)
                rim = jnp.where(row < 6, pltpu.roll(kv[h, a, 1, n, 0].astype(F32), 4, 0), rim)
                rim = jnp.where(row < 4, pltpu.roll(kv[h, a, nc, n, 1].astype(F32), 4, 0), rim)
                rims.append(jnp.where(row < 2, pltpu.roll(kv[h, a, nc, n, 0].astype(F32), 2, 0), rim))
            for k in range(per_half):
                tile = jnp.concatenate([r[:, k * part:(k + 1) * part] for r in rims * folds], axis=1)
                xs[halves * k + h, a, LANES:LANES + rows, :] = tile.astype(BF16)

            for d in (2, 1, 3, 0):
                p = halves * lax.rem(z // halves + d, per_half) + h

                def send_x(p=p, a=a):
                    pltpu.make_async_remote_copy(
                        src_ref=xs.at[p, a], dst_ref=xr.at[z, a], send_sem=x_s, recv_sem=x_r.at[z, a],
                        device_id=(p, c), device_id_type=MESH).start()

                if d > 0:
                    send_x()
                else:
                    pl.when(own_half != h)(send_x)

            if (h, a) == (halves - 1, 0):
                each_partner(send_q)

            @pl.when(own_half == h)
            def _():
                pltpu.make_async_copy(xs.at[z, a], xr.at[z, a], x_r.at[z, a]).start()

    def pass_query_rim():
        settle(qb.at[nc], q_r.at[1])

        @pl.when(z < nz - 1)
        def _():
            pltpu.make_async_remote_copy(
                src_ref=qb.at[nc], dst_ref=qb.at[0], send_sem=h_s, recv_sem=h_r,
                device_id=(z + 1, c), device_id_type=MESH).start()

    pl.when(own_half != 0)(pass_query_rim)

    before = None
    for s in range(nz):
        tiles, rims = [], []
        for a in range(pairs):
            settle(xr.at[s, a], x_r.at[s, a])
            tiles.append(xr[s, a, :LANES, :])
            rims.append(xr[s, a, LANES:LANES + rows, :].astype(F32)[:, :LANES // pairs])
        for f in range(folds):
            at = f * LANES // folds
            xu[nz - 1 - s, f * LANES:(f + 1) * LANES, :] = jnp.concatenate(
                [t[:, at:at + LANES // folds] for t in tiles], axis=1)
        rim = jnp.concatenate(rims, axis=1)
        if s > 0:
            firsts, seconds = [], []
            for i in range(2):
                t0, t1 = rim[4 + 2 * i:5 + 2 * i], rim[5 + 2 * i:6 + 2 * i]
                b2, b1 = before[2 * i:2 * i + 1], before[2 * i + 1:2 * i + 2]
                w0, w1, w2 = wl[0, i, 0:1], wl[1, i, 0:1], wl[2, i, 0:1]
                firsts.append(w0 * t0 + w1 * b1 + w2 * b2)
                seconds.append(w0 * t1 + w1 * t0 + w2 * b1)
            head = xu[nz - 1 - s, 0:2 * rows, :].astype(F32)
            at = lax.broadcasted_iota(jnp.int32, head.shape, 0)
            head = jnp.where(at == 0, firsts[0] * firsts[1], head)
            head = jnp.where(at == 1, seconds[0] * seconds[1], head)
            xu[nz - 1 - s, 0:2 * rows, :] = head.astype(BF16)
        before = rim

    lane = lax.broadcasted_iota(jnp.int32, (1, 2 * LANES), 1)
    for m in range(nz // 2):
        lags = 2 * m + 2
        even = xu[nz - 1 - 2 * m:nz - 1 - 2 * m + lags].reshape(lags * block, LANES)
        odd = xu[nz - 2 - 2 * m:nz - 2 - 2 * m + lags].reshape(lags * block, LANES)
        both = jnp.concatenate([even, odd], axis=1)
        total = None
        for g in range(groups):
            keep = ((lane // GSIZE) % groups == g).astype(F32).astype(BF16)
            term = jnp.dot(toep[g, :, 0:lags * block], both * keep, preferred_element_type=F32)
            total = term if total is None else total + term
        ys[2 * m] = total[:, :LANES].astype(BF16)
        ys[2 * m + 1] = total[:, LANES:].astype(BF16)

    for d in line:
        p = lax.rem(z + d, nz)
        pltpu.make_async_remote_copy(
            src_ref=ys.at[p], dst_ref=yr.at[z], send_sem=y_s, recv_sem=y_r.at[z],
            device_id=(p, c), device_id_type=MESH).start()
    pltpu.make_async_copy(ys.at[z], yr.at[z], y_r.at[z]).start()

    pl.when(own_half == 0)(pass_query_rim)
    settle(qb.at[1:nc], q_r.at[0])

    @pl.when(z > 0)
    def _():
        settle(qb.at[0], h_r)

    def query_chunk(j, carry):
        s0 = j * chunk
        for h in range(halves):
            for n in range(seqs):
                ext = qb[pl.ds(s0, chunk + 1), n, :, h * LANES:(h + 1) * LANES].astype(F32)
                value = feature(ext.reshape((chunk + 1) * rows, LANES), 0, h)
                qf[pl.ds(s0, chunk), n, :, h * LANES:(h + 1) * LANES] = value.astype(BF16).reshape(
                    chunk, rows, LANES)
        return carry

    lax.fori_loop(0, chunks, query_chunk, 0)

    for h in range(halves):
        for k in range(per_half):
            settle(yr.at[halves * k + h], y_r.at[halves * k + h])

        def gate_chunk(j, carry, h=h):
            s0 = j * chunk
            t0 = pl.multiple_of(j * span, span)
            tiles = [yr[halves * k + h, pl.ds(t0, span), :].astype(F32) for k in range(per_half)]
            for n in range(seqs):
                filtered = jnp.concatenate([t[:, n * part:(n + 1) * part] for t in tiles], axis=1)
                query = qf[pl.ds(s0, chunk), n, :, h * LANES:(h + 1) * LANES].astype(F32)
                gated = query * filtered.reshape(chunk, rows, LANES)
                gs[h, pl.ds(s0, chunk), n] = gated.astype(BF16)
            return carry

        lax.fori_loop(0, chunks, gate_chunk, 0)

        def send_out(p, h=h):
            pltpu.make_async_remote_copy(
                src_ref=gs.at[h, p], dst_ref=out.at[:, :, half_cols(c, h)], send_sem=o_s, recv_sem=o_r,
                device_id=(z, p), device_id_type=MESH).start()

        each_partner(send_out)
        pltpu.make_async_copy(gs.at[h, c], out.at[:, :, half_cols(c, h)], o_r).start()

    settle(kv.at[:, :, 1:nc], kv_s)
    settle(qb.at[1:nc], q_s)
    settle(xs.at[1:nz], x_s)
    settle(ys.at[1:nz], y_s)

    @pl.when(z < nz - 1)
    def _():
        settle(qb.at[nc], h_s)

    settle(gs.at[:, 1:nc], o_s)
    settle(out, o_r)


def solution(mesh):
    nz, nc = mesh.shape["seq"], mesh.shape["ch"]

    def shards(proj, short_w, long_filter):
        seqs, rows, _, width = proj.shape
        chans = width // nc
        block = rows * nc
        halves = chans // LANES
        part = chans // nz
        pairs = seqs * part // LANES * (block // LANES)
        groups, length = long_filter.shape
        own = part // GSIZE
        by_component = jnp.transpose(proj, (0, 2, 1, 3))
        dma = pltpu.SemaphoreType.DMA
        sources = pltpu.VMEM((nz, pairs, LANES + rows, LANES), BF16)
        results = pltpu.VMEM((nz, block, LANES), BF16)
        duo = seqs // pairs
        return pl.pallas_call(
            lambda *refs: kernel(nz, nc, *refs),
            out_shape=jax.ShapeDtypeStruct((seqs, rows, width), BF16),
            in_specs=[pl.BlockSpec(memory_space=pl.ANY)] * 3,
            out_specs=pl.BlockSpec(memory_space=pl.ANY),
            scratch_shapes=[
                pltpu.VMEM((seqs, 3, rows, width), BF16),
                pltpu.VMEM(short_w.shape, F32),
                pltpu.VMEM(long_filter.shape, BF16),
                pltpu.VMEM((halves, pairs, nc + 1, duo, 2, rows, LANES), BF16),
                pltpu.VMEM((nc + 1, seqs, rows, chans), BF16),
                pltpu.VMEM((nc, seqs, rows, chans), BF16),
                sources, sources,
                pltpu.VMEM((nz + 1, block, LANES), BF16),
                pltpu.VMEM((short_w.shape[0], 2, rows, LANES), F32),
                results, results,
                pltpu.VMEM((halves, nc, seqs, rows, LANES), BF16),
                pltpu.VMEM((own, block, length), BF16),
                pltpu.VMEM((groups, length + LANES), F32),
                dma((3,)), dma, dma((halves, pairs)), dma, dma((2,)), dma, dma,
                dma, dma((nz, pairs)), dma, dma((nz,)), dma, dma,
            ],
            compiler_params=pltpu.CompilerParams(collective_id=0, has_side_effects=True),
            name="hyena",
        )(by_component, short_w, long_filter)

    in_specs = (P(None, ("seq", "ch"), None, None), P(None, None, "ch"), P("ch", None))
    out_specs = P(None, ("seq", "ch"), None)
    return jax.shard_map(shards, mesh=mesh, in_specs=in_specs, out_specs=out_specs, check_vma=False)
```

```python
import jax
import jax.numpy as jnp
from jax import lax
from jax.experimental import pallas as pl
from jax.experimental.pallas import tpu as pltpu
from jax.sharding import PartitionSpec as P

MESH = pl.DeviceIdType.MESH
GSIZE = 16
LANES = 128
F32 = jnp.float32
BF16 = jnp.bfloat16


def kernel(nz, nc, proj_in, w_in, lf_in, out, proj, w_ref, lf_ref, kv, qb, qf, xs, xr, xu, edge, wl, ys, yr, gs, toep, rev,
           in_r, kv_s, kv_r, q_s, q_r, h_s, h_r, x_s, x_r, y_s, y_r, o_s, o_r):
    z = lax.axis_index("seq")
    c = lax.axis_index("ch")
    seqs, _, rows, _ = proj.shape
    halves, pairs, chans = kv.shape[0], kv.shape[1], qb.shape[-1]
    duo = seqs // pairs
    block = rows * nc
    part = chans // nz
    per_half = LANES // part
    taps = w_ref.shape[0]
    chunk = 8
    chunks = nc // chunk
    span = chunk * rows
    folds = block // LANES
    fold_slots = nc // folds
    strips = fold_slots // chunk
    own_half = lax.rem(z + c, halves)
    parity = [lax.rem(h + c, halves) for h in range(halves)]
    side = 4
    around = (2, 1, 3, 0)
    line = (4, 3, 5, 2, 6, 1, 7)

    def cols(p):
        return pl.ds(pl.multiple_of(p * chans, chans), chans)

    def half_cols(p, h):
        return pl.ds(pl.multiple_of(p * chans + h * LANES, LANES), LANES)

    def settle(ref, sem):
        pltpu.make_async_copy(ref, ref, sem).wait()

    across = [lax.rem(c // 8 + d, side) * 8 for d in range(side)]
    along = [lax.rem(c // 2 + d, side) * 2 for d in range(side)]
    core = [lax.rem(c + d, 2) for d in range(2)]

    def each_partner(body):
        for dx in around:
            for dy in around:
                for dc in (1, 0):
                    if (dx, dy, dc) != (0, 0, 0):
                        body(across[dx] + along[dy] + core[dc])

    barrier = pltpu.get_barrier_semaphore()

    def greet(p):
        pl.semaphore_signal(barrier, inc=1, device_id=(z, p), device_id_type=MESH)

    for n in range(seqs):
        pltpu.make_async_copy(proj_in.at[n], proj.at[n], in_r.at[0]).start()
    pltpu.make_async_copy(lf_in, lf_ref, in_r.at[1]).start()
    pltpu.make_async_copy(w_in, w_ref, in_r.at[2]).start()
    each_partner(greet)
    for d in line:
        pl.semaphore_signal(barrier, inc=1, device_id=(lax.rem(z + d, nz), c), device_id_type=MESH)
    settle(proj, in_r.at[0])
    last = c // (nc - 1)
    for h in range(halves):
        for a in range(pairs):
            pltpu.make_async_copy(
                proj.at[a * duo:(a + 1) * duo, 1:3, :, half_cols(c, h)], kv.at[h, a, c + 1],
                kv_r.at[h, a]).start()
    pltpu.make_async_copy(proj.at[:, 0, :, cols(c)], qb.at[c + 1], q_r.at[last]).start()
    pl.semaphore_wait(barrier, nc - 1 + nz - 1)

    for h in range(halves):
        for a in range(pairs):
            def send_kv(p, h=h, a=a):
                pltpu.make_async_remote_copy(
                    src_ref=proj.at[a * duo:(a + 1) * duo, 1:3, :, half_cols(p, h)],
                    dst_ref=kv.at[h, a, c + 1], send_sem=kv_s, recv_sem=kv_r.at[h, a],
                    device_id=(z, p), device_id_type=MESH).start()

            each_partner(send_kv)

    settle(lf_ref, in_r.at[1])
    settle(w_ref, in_r.at[2])

    length = lf_ref.shape[1]
    pieces = length // LANES
    flip = (lax.broadcasted_iota(jnp.int32, (LANES, LANES), 0)
            + lax.broadcasted_iota(jnp.int32, (LANES, LANES), 1)) == LANES - 1
    flip = flip.astype(F32).astype(BF16)
    rev[:, 0:LANES] = jnp.zeros((lf_ref.shape[0], LANES), F32)
    for m in range(pieces):
        rev[:, (m + 1) * LANES:(m + 2) * LANES] = jnp.dot(
            lf_ref[:, m * LANES:(m + 1) * LANES], flip, preferred_element_type=F32)
    groups = part // GSIZE
    own_row = (own_half * LANES + (z // halves) * part) // GSIZE
    for g in range(groups):
        for m in range(pieces):
            pair = rev[pl.ds(own_row + g, 1), m * LANES:(m + 2) * LANES]
            pair = jnp.broadcast_to(pair, (LANES, 2 * LANES))
            tile = pltpu.roll(pair, 1, 1, stride=1, stride_axis=0)[:, :LANES]
            tile = tile.astype(BF16)
            for th in range(2):
                for sh in range(2):
                    twice = m - th + sh
                    if twice % 2 == 0 and 0 <= twice // 2 < nz:
                        base = (twice // 2) * block + sh * LANES
                        toep[g, th * LANES:(th + 1) * LANES, base:base + LANES] = tile
        toep[g, 0:LANES, LANES:2 * LANES] = jnp.zeros((LANES, LANES), BF16)

    for k in range(taps):
        for i in range(2):
            mine = jnp.where(own_half == 0, w_ref[k, i + 1:i + 2, :LANES], w_ref[k, i + 1:i + 2, LANES:])
            mine = pltpu.roll(jnp.broadcast_to(mine, (rows, LANES)), LANES - (z // halves) * part, 1)
            wl[k, i] = jnp.concatenate([mine[:, :part]] * seqs, axis=1)

    xu[nz] = jnp.zeros(xu.shape[1:], BF16)
    row = lax.broadcasted_iota(jnp.int32, (rows, LANES), 0)
    for h in range(halves):
        for a in range(pairs):
            kv[h, a, 0] = jnp.zeros(kv.shape[3:], BF16)

    @pl.when(z == 0)
    def _():
        qb[0] = jnp.zeros(qb.shape[1:], BF16)

    def feature(ext, i, h):
        total = None
        for k in range(taps):
            term = w_ref[k, i:i + 1, h * LANES:(h + 1) * LANES] * ext[rows - k:rows - k + span]
            total = term if total is None else total + term
        return total

    def send_q(p):
        pltpu.make_async_remote_copy(
            src_ref=proj.at[:, 0, :, cols(p)], dst_ref=qb.at[c + 1], send_sem=q_s,
            recv_sem=q_r.at[last], device_id=(z, p), device_id_type=MESH).start()

    for h in range(halves):
        for a in range(pairs):
            settle(kv.at[h, a, 1:nc + 1], kv_r.at[h, a])

            def product_strip(k, carry, h=h, a=a):
                j = strips - 1 - k

                prods = []
                for f in range(folds):
                    for n in range(duo):
                        feats = []
                        for i in range(2):
                            ext = kv[h, a, pl.ds(f * fold_slots + j * chunk, chunk + 1), n, i].astype(F32)
                            feats.append(feature(ext.reshape((chunk + 1) * rows, LANES), i + 1, h))
                        prods.append(feats[0] * feats[1])
                t0 = pl.multiple_of(j * span, span)
                for k in range(per_half):
                    tile = jnp.concatenate([p[:, k * part:(k + 1) * part] for p in prods], axis=1)
                    xs[halves * k + parity[h], a, pl.ds(t0, span), :] = tile.astype(BF16)
                return carry

            lax.fori_loop(0, strips, product_strip, 0)

            rims = []
            for n in range(duo):
                rim = pltpu.roll(kv[h, a, 1, n, 1].astype(F32), 6, 0)
                rim = jnp.where(row < 6, pltpu.roll(kv[h, a, 1, n, 0].astype(F32), 4, 0), rim)
                rim = jnp.where(row < 4, pltpu.roll(kv[h, a, nc, n, 1].astype(F32), 4, 0), rim)
                rims.append(jnp.where(row < 2, pltpu.roll(kv[h, a, nc, n, 0].astype(F32), 2, 0), rim))
            for k in range(per_half):
                tile = jnp.concatenate([r[:, k * part:(k + 1) * part] for r in rims * folds], axis=1)
                xs[halves * k + parity[h], a, LANES:LANES + rows, :] = tile.astype(BF16)

            for d in (2, 1, 3, 0):
                p = halves * lax.rem(z // halves + d, per_half) + parity[h]

                def send_x(p=p, a=a):
                    pltpu.make_async_remote_copy(
                        src_ref=xs.at[p, a], dst_ref=xr.at[z, a], send_sem=x_s, recv_sem=x_r.at[z, a],
                        device_id=(p, c), device_id_type=MESH).start()

                if d > 0:
                    send_x()
                else:
                    pl.when(own_half != h)(send_x)

            if (h, a) == (halves - 1, 0):
                each_partner(send_q)

            @pl.when(own_half == h)
            def _():
                pltpu.make_async_copy(xs.at[z, a], xr.at[z, a], x_r.at[z, a]).start()

    for s in range(nz):
        for a in range(pairs):
            settle(xr.at[s, a], x_r.at[s, a])
    for s in range(nz):
        tiles = [xr[s, a, :LANES, :] for a in range(pairs)]
        rims = [xr[s, a, LANES:LANES + rows, :].astype(F32)[:, :LANES // pairs] for a in range(pairs)]
        for f in range(folds):
            at = f * LANES // folds
            xu[nz - 1 - s, f * LANES:(f + 1) * LANES, :] = jnp.concatenate(
                [t[:, at:at + LANES // folds] for t in tiles], axis=1)
        edge[s] = jnp.concatenate(rims, axis=1)

    firsts, seconds = [], []
    for i in range(2):
        b2, b1 = edge[:, 2 * i, :], edge[:, 2 * i + 1, :]
        t0, t1 = edge[:, 4 + 2 * i, :], edge[:, 5 + 2 * i, :]
        block_row = lax.broadcasted_iota(jnp.int32, b2.shape, 0)
        b2 = jnp.where(block_row == 0, 0.0, pltpu.roll(b2, 1, 0))
        b1 = jnp.where(block_row == 0, 0.0, pltpu.roll(b1, 1, 0))
        w0, w1, w2 = wl[0, i], wl[1, i], wl[2, i]
        firsts.append(w0 * t0 + w1 * b1 + w2 * b2)
        seconds.append(w0 * t1 + w1 * t0 + w2 * b1)
    first, second = firsts[0] * firsts[1], seconds[0] * seconds[1]
    for s in range(1, nz):
        head = xu[nz - 1 - s, 0:2 * rows, :].astype(F32)
        at = lax.broadcasted_iota(jnp.int32, head.shape, 0)
        head = jnp.where(at == 0, first[s:s + 1], jnp.where(at == 1, second[s:s + 1], head))
        xu[nz - 1 - s, 0:2 * rows, :] = head.astype(BF16)

    lane = lax.broadcasted_iota(jnp.int32, (1, 2 * LANES), 1)
    for m in range(nz // 2):
        lags = 2 * m + 2
        even = xu[nz - 1 - 2 * m:nz - 1 - 2 * m + lags].reshape(lags * block, LANES)
        odd = xu[nz - 2 - 2 * m:nz - 2 - 2 * m + lags].reshape(lags * block, LANES)
        both = jnp.concatenate([even, odd], axis=1)
        total = None
        for g in range(groups):
            keep = ((lane // GSIZE) % groups == g).astype(F32).astype(BF16)
            term = jnp.dot(toep[g, :, 0:lags * block], both * keep, preferred_element_type=F32)
            total = term if total is None else total + term
        ys[2 * m] = total[:, :LANES].astype(BF16)
        ys[2 * m + 1] = total[:, LANES:].astype(BF16)
        if m == 1:
            settle(qb.at[nc], q_r.at[1])

            @pl.when(z < nz - 1)
            def _():
                pltpu.make_async_remote_copy(
                    src_ref=qb.at[nc], dst_ref=qb.at[0], send_sem=h_s, recv_sem=h_r,
                    device_id=(z + 1, c), device_id_type=MESH).start()

        if m % 2 == 1:
            for p in range(2 * m - 2, 2 * m + 2):
                @pl.when(z != p)
                def _(p=p):
                    pltpu.make_async_remote_copy(
                        src_ref=ys.at[p], dst_ref=yr.at[z], send_sem=y_s, recv_sem=y_r.at[z],
                        device_id=(p, c), device_id_type=MESH).start()
    pltpu.make_async_copy(ys.at[z], yr.at[z], y_r.at[z]).start()

    settle(qb.at[1:nc], q_r.at[0])

    @pl.when(z > 0)
    def _():
        settle(qb.at[0], h_r)

    def query_chunk(j, carry):
        s0 = j * chunk
        for h in range(halves):
            for n in range(seqs):
                ext = qb[pl.ds(s0, chunk + 1), n, :, h * LANES:(h + 1) * LANES].astype(F32)
                value = feature(ext.reshape((chunk + 1) * rows, LANES), 0, h)
                qf[pl.ds(s0, chunk), n, :, h * LANES:(h + 1) * LANES] = value.astype(BF16).reshape(
                    chunk, rows, LANES)
        return carry

    lax.fori_loop(0, chunks, query_chunk, 0)

    for h in range(halves):
        for k in range(per_half):
            settle(yr.at[halves * k + parity[h]], y_r.at[halves * k + parity[h]])

        def gate_chunk(j, carry, h=h):
            s0 = j * chunk
            t0 = pl.multiple_of(j * span, span)
            tiles = [yr[halves * k + parity[h], pl.ds(t0, span), :].astype(F32) for k in range(per_half)]
            for n in range(seqs):
                filtered = jnp.concatenate([t[:, n * part:(n + 1) * part] for t in tiles], axis=1)
                query = qf[pl.ds(s0, chunk), n, :, h * LANES:(h + 1) * LANES].astype(F32)
                gated = query * filtered.reshape(chunk, rows, LANES)
                gs[h, pl.ds(s0, chunk), n] = gated.astype(BF16)
            return carry

        lax.fori_loop(0, chunks, gate_chunk, 0)

        def send_out(p, h=h):
            pltpu.make_async_remote_copy(
                src_ref=gs.at[h, p], dst_ref=out.at[:, :, half_cols(c, h)], send_sem=o_s, recv_sem=o_r,
                device_id=(z, p), device_id_type=MESH).start()

        each_partner(send_out)
        pltpu.make_async_copy(gs.at[h, c], out.at[:, :, half_cols(c, h)], o_r).start()

    settle(kv.at[:, :, 1:nc], kv_s)
    settle(qb.at[1:nc], q_s)
    settle(xs.at[1:nz], x_s)
    settle(ys.at[1:nz], y_s)

    @pl.when(z < nz - 1)
    def _():
        settle(qb.at[nc], h_s)

    settle(gs.at[:, 1:nc], o_s)
    settle(out, o_r)


def solution(mesh):
    nz, nc = mesh.shape["seq"], mesh.shape["ch"]

    def shards(proj, short_w, long_filter):
        seqs, rows, _, width = proj.shape
        chans = width // nc
        block = rows * nc
        halves = chans // LANES
        part = chans // nz
        pairs = seqs * part // LANES * (block // LANES)
        groups, length = long_filter.shape
        own = part // GSIZE
        by_component = jnp.transpose(proj, (0, 2, 1, 3))
        dma = pltpu.SemaphoreType.DMA
        sources = pltpu.VMEM((nz, pairs, LANES + rows, LANES), BF16)
        results = pltpu.VMEM((nz, block, LANES), BF16)
        duo = seqs // pairs
        return pl.pallas_call(
            lambda *refs: kernel(nz, nc, *refs),
            out_shape=pltpu.VMEM((seqs, rows, width), BF16),
            in_specs=[pl.BlockSpec(memory_space=pltpu.HBM)] * 3,
            out_specs=pl.BlockSpec(memory_space=pl.ANY),
            scratch_shapes=[
                pltpu.VMEM((seqs, 3, rows, width), BF16),
                pltpu.VMEM(short_w.shape, F32),
                pltpu.VMEM(long_filter.shape, BF16),
                pltpu.VMEM((halves, pairs, nc + 1, duo, 2, rows, LANES), BF16),
                pltpu.VMEM((nc + 1, seqs, rows, chans), BF16),
                pltpu.VMEM((nc, seqs, rows, chans), BF16),
                sources, sources,
                pltpu.VMEM((nz + 1, block, LANES), BF16),
                pltpu.VMEM((nz, rows, LANES), F32),
                pltpu.VMEM((short_w.shape[0], 2, rows, LANES), F32),
                results, results,
                pltpu.VMEM((halves, nc, seqs, rows, LANES), BF16),
                pltpu.VMEM((own, block, length), BF16),
                pltpu.VMEM((groups, length + LANES), F32),
                dma((3,)), dma, dma((halves, pairs)), dma, dma((2,)), dma, dma,
                dma, dma((nz, pairs)), dma, dma((nz,)), dma, dma,
            ],
            compiler_params=pltpu.CompilerParams(collective_id=0, has_side_effects=True),
            name="hyena",
        )(by_component, short_w, long_filter)

    in_specs = (P(None, ("seq", "ch"), None, None), P(None, None, "ch"), P("ch", None))
    out_specs = P(None, ("seq", "ch"), None)
    return jax.shard_map(shards, mesh=mesh, in_specs=in_specs, out_specs=out_specs, check_vma=False)
```

```python
import jax
import jax.numpy as jnp
from jax import lax
from jax.experimental import pallas as pl
from jax.experimental.pallas import tpu as pltpu
from jax.sharding import PartitionSpec as P

MESH = pl.DeviceIdType.MESH
GSIZE = 16
LANES = 128
F32 = jnp.float32
BF16 = jnp.bfloat16


def kernel(nz, nc, proj_in, w_in, lf_in, out, proj, w_ref, lf_ref, kv, qb, qf, xs, xr, xu, edge, wl, ys, yr, gs, toep, rev,
           in_r, kv_s, kv_r, q_s, q_r, h_s, h_r, x_s, x_r, y_s, y_r, o_s, o_r):
    z = lax.axis_index("seq")
    c = lax.axis_index("ch")
    seqs, _, rows, _ = proj.shape
    halves, pairs, chans = kv.shape[0], kv.shape[1], qb.shape[-1]
    duo = seqs // pairs
    block = rows * nc
    part = chans // nz
    per_half = LANES // part
    taps = w_ref.shape[0]
    chunk = 8
    chunks = nc // chunk
    span = chunk * rows
    folds = block // LANES
    fold_slots = nc // folds
    strips = fold_slots // chunk
    own_half = lax.rem(z + c, halves)
    parity = [lax.rem(h + c, halves) for h in range(halves)]
    side = 4
    around = (2, 1, 3, 0)
    line = (4, 3, 5, 2, 6, 1, 7)

    def cols(p):
        return pl.ds(pl.multiple_of(p * chans, chans), chans)

    def half_cols(p, h):
        return pl.ds(pl.multiple_of(p * chans + h * LANES, LANES), LANES)

    def settle(ref, sem):
        pltpu.make_async_copy(ref, ref, sem).wait()

    across = [lax.rem(c // 8 + d, side) * 8 for d in range(side)]
    along = [lax.rem(c // 2 + d, side) * 2 for d in range(side)]
    core = [lax.rem(c + d, 2) for d in range(2)]

    def each_partner(body):
        for dx in around:
            for dy in around:
                for dc in (1, 0):
                    if (dx, dy, dc) != (0, 0, 0):
                        body(across[dx] + along[dy] + core[dc])

    barrier = pltpu.get_barrier_semaphore()

    def greet(p):
        pl.semaphore_signal(barrier, inc=1, device_id=(z, p), device_id_type=MESH)

    for n in range(seqs):
        pltpu.make_async_copy(proj_in.at[n], proj.at[n], in_r.at[0]).start()
    pltpu.make_async_copy(lf_in, lf_ref, in_r.at[1]).start()
    pltpu.make_async_copy(w_in, w_ref, in_r.at[2]).start()
    each_partner(greet)
    for d in line:
        pl.semaphore_signal(barrier, inc=1, device_id=(lax.rem(z + d, nz), c), device_id_type=MESH)
    settle(proj, in_r.at[0])
    last = c // (nc - 1)
    for h in range(halves):
        for a in range(pairs):
            pltpu.make_async_copy(
                proj.at[a * duo:(a + 1) * duo, 1:3, :, half_cols(c, h)], kv.at[h, a, c + 1],
                kv_r.at[h, a]).start()
    pltpu.make_async_copy(proj.at[:, 0, :, cols(c)], qb.at[c + 1], q_r.at[last]).start()
    pl.semaphore_wait(barrier, nc - 1 + nz - 1)

    for h in range(halves):
        for a in range(pairs):
            def send_kv(p, h=h, a=a):
                pltpu.make_async_remote_copy(
                    src_ref=proj.at[a * duo:(a + 1) * duo, 1:3, :, half_cols(p, h)],
                    dst_ref=kv.at[h, a, c + 1], send_sem=kv_s, recv_sem=kv_r.at[h, a],
                    device_id=(z, p), device_id_type=MESH).start()

            each_partner(send_kv)

    settle(lf_ref, in_r.at[1])
    settle(w_ref, in_r.at[2])

    length = lf_ref.shape[1]
    pieces = length // LANES
    flip = (lax.broadcasted_iota(jnp.int32, (LANES, LANES), 0)
            + lax.broadcasted_iota(jnp.int32, (LANES, LANES), 1)) == LANES - 1
    flip = flip.astype(F32).astype(BF16)
    rev[:, 0:LANES] = jnp.zeros((lf_ref.shape[0], LANES), F32)
    for m in range(pieces):
        rev[:, (m + 1) * LANES:(m + 2) * LANES] = jnp.dot(
            lf_ref[:, m * LANES:(m + 1) * LANES], flip, preferred_element_type=F32)
    groups = part // GSIZE
    own_row = (own_half * LANES + (z // halves) * part) // GSIZE
    for g in range(groups):
        for m in range(pieces):
            pair = rev[pl.ds(own_row + g, 1), m * LANES:(m + 2) * LANES]
            pair = jnp.broadcast_to(pair, (LANES, 2 * LANES))
            tile = pltpu.roll(pair, 1, 1, stride=1, stride_axis=0)[:, :LANES]
            tile = tile.astype(BF16)
            for th in range(2):
                for sh in range(2):
                    twice = m - th + sh
                    if twice % 2 == 0 and 0 <= twice // 2 < nz:
                        base = (twice // 2) * block + sh * LANES
                        toep[g, th * LANES:(th + 1) * LANES, base:base + LANES] = tile
        toep[g, 0:LANES, LANES:2 * LANES] = jnp.zeros((LANES, LANES), BF16)

    for k in range(taps):
        for i in range(2):
            mine = jnp.where(own_half == 0, w_ref[k, i + 1:i + 2, :LANES], w_ref[k, i + 1:i + 2, LANES:])
            mine = pltpu.roll(jnp.broadcast_to(mine, (rows, LANES)), LANES - (z // halves) * part, 1)
            wl[k, i] = jnp.concatenate([mine[:, :part]] * seqs, axis=1)

    xu[nz] = jnp.zeros(xu.shape[1:], BF16)
    row = lax.broadcasted_iota(jnp.int32, (rows, LANES), 0)
    for h in range(halves):
        for a in range(pairs):
            kv[h, a, 0] = jnp.zeros(kv.shape[3:], BF16)

    @pl.when(z == 0)
    def _():
        qb[0] = jnp.zeros(qb.shape[1:], BF16)

    def feature(ext, i, h):
        total = None
        for k in range(taps):
            term = w_ref[k, i:i + 1, h * LANES:(h + 1) * LANES] * ext[rows - k:rows - k + span]
            total = term if total is None else total + term
        return total

    def send_q(p):
        pltpu.make_async_remote_copy(
            src_ref=proj.at[:, 0, :, cols(p)], dst_ref=qb.at[c + 1], send_sem=q_s,
            recv_sem=q_r.at[last], device_id=(z, p), device_id_type=MESH).start()

    for h in range(halves):
        for a in range(pairs):
            settle(kv.at[h, a, 1:nc + 1], kv_r.at[h, a])

            def product_strip(k, carry, h=h, a=a):
                j = strips - 1 - k

                prods = []
                for f in range(folds):
                    for n in range(duo):
                        feats = []
                        for i in range(2):
                            ext = kv[h, a, pl.ds(f * fold_slots + j * chunk, chunk + 1), n, i].astype(F32)
                            feats.append(feature(ext.reshape((chunk + 1) * rows, LANES), i + 1, h))
                        prods.append(feats[0] * feats[1])
                t0 = pl.multiple_of(j * span, span)
                for k in range(per_half):
                    tile = jnp.concatenate([p[:, k * part:(k + 1) * part] for p in prods], axis=1)
                    xs[halves * k + parity[h], a, pl.ds(t0, span), :] = tile.astype(BF16)
                return carry

            lax.fori_loop(0, strips, product_strip, 0)

            tall = LANES
            if a == pairs - 1:
                tall = LANES + rows
                rims = []
                for n in range(seqs):
                    head, tail = kv.at[h, n // duo, 1, n % duo], kv.at[h, n // duo, nc, n % duo]
                    rim = pltpu.roll(head[1].astype(F32), 6, 0)
                    rim = jnp.where(row < 6, pltpu.roll(head[0].astype(F32), 4, 0), rim)
                    rim = jnp.where(row < 4, pltpu.roll(tail[1].astype(F32), 4, 0), rim)
                    rims.append(jnp.where(row < 2, pltpu.roll(tail[0].astype(F32), 2, 0), rim))
                for k in range(per_half):
                    tile = jnp.concatenate([r[:, k * part:(k + 1) * part] for r in rims], axis=1)
                    xs[halves * k + parity[h], a, LANES:LANES + rows, :] = tile.astype(BF16)

            for d in (2, 1, 3, 0):
                p = halves * lax.rem(z // halves + d, per_half) + parity[h]

                def send_x(p=p, a=a, tall=tall):
                    pltpu.make_async_remote_copy(
                        src_ref=xs.at[p, a, 0:tall], dst_ref=xr.at[z, a, 0:tall], send_sem=x_s, recv_sem=x_r.at[z, a],
                        device_id=(p, c), device_id_type=MESH).start()

                if d > 0:
                    send_x()
                else:
                    pl.when(own_half != h)(send_x)

            if (h, a) == (halves - 1, 0):
                each_partner(send_q)

            @pl.when(own_half == h)
            def _():
                pltpu.make_async_copy(
                    xs.at[z, a, 0:tall], xr.at[z, a, 0:tall], x_r.at[z, a]).start()

    def pass_query_rim():
        settle(qb.at[nc], q_r.at[1])

        @pl.when(z < nz - 1)
        def _():
            pltpu.make_async_remote_copy(
                src_ref=qb.at[nc], dst_ref=qb.at[0], send_sem=h_s, recv_sem=h_r,
                device_id=(z + 1, c), device_id_type=MESH).start()

    pl.when(own_half != 0)(pass_query_rim)

    for s in range(nz):
        for a in range(pairs):
            settle(xr.at[s, a, 0:LANES + rows * (a // (pairs - 1))], x_r.at[s, a])
    for s in range(nz):
        tiles = [xr[s, a, :LANES, :] for a in range(pairs)]
        for f in range(folds):
            at = f * LANES // folds
            xu[nz - 1 - s, f * LANES:(f + 1) * LANES, :] = jnp.concatenate(
                [t[:, at:at + LANES // folds] for t in tiles], axis=1)
        edge[s] = xr[s, pairs - 1, LANES:LANES + rows, :].astype(F32)

    firsts, seconds = [], []
    for i in range(2):
        b2, b1 = edge[:, 2 * i, :], edge[:, 2 * i + 1, :]
        t0, t1 = edge[:, 4 + 2 * i, :], edge[:, 5 + 2 * i, :]
        block_row = lax.broadcasted_iota(jnp.int32, b2.shape, 0)
        b2 = jnp.where(block_row == 0, 0.0, pltpu.roll(b2, 1, 0))
        b1 = jnp.where(block_row == 0, 0.0, pltpu.roll(b1, 1, 0))
        w0, w1, w2 = wl[0, i], wl[1, i], wl[2, i]
        firsts.append(w0 * t0 + w1 * b1 + w2 * b2)
        seconds.append(w0 * t1 + w1 * t0 + w2 * b1)
    first, second = firsts[0] * firsts[1], seconds[0] * seconds[1]
    for s in range(1, nz):
        head = xu[nz - 1 - s, 0:2 * rows, :].astype(F32)
        at = lax.broadcasted_iota(jnp.int32, head.shape, 0)
        head = jnp.where(at == 0, first[s:s + 1], jnp.where(at == 1, second[s:s + 1], head))
        xu[nz - 1 - s, 0:2 * rows, :] = head.astype(BF16)

    lane = lax.broadcasted_iota(jnp.int32, (1, 2 * LANES), 1)

    def send_y(p, e):
        @pl.when(z != p)
        def _():
            pltpu.make_async_remote_copy(
                src_ref=ys.at[p, e], dst_ref=yr.at[z, e], send_sem=y_s, recv_sem=y_r.at[z, e],
                device_id=(p, c), device_id_type=MESH).start()

    for m in range(nz // 2):
        lags = 2 * m + 2
        even = xu[nz - 1 - 2 * m:nz - 1 - 2 * m + lags].reshape(lags * block, LANES)
        odd = xu[nz - 2 - 2 * m:nz - 2 - 2 * m + lags].reshape(lags * block, LANES)
        both = jnp.concatenate([even, odd], axis=1)
        total = None
        for g in range(groups):
            keep = ((lane // GSIZE) % groups == g).astype(F32).astype(BF16)
            term = jnp.dot(toep[g, :, 0:lags * block], both * keep, preferred_element_type=F32)
            total = term if total is None else total + term
        for i in range(2):
            result = total[:, i * LANES:(i + 1) * LANES].astype(BF16)
            result = result.reshape(nc // 2, 2, rows, LANES)
            for e in range(2):
                ys[2 * m + i, e] = result[:, e]
        if m == nz // 2 - 1:
            pl.when(own_half == 0)(pass_query_rim)
        if m % 2 == 1:
            for p in range(2 * m - 2, 2 * m + 2):
                send_y(p, 0)
    for p in range(nz):
        send_y(p, 1)
    for e in range(2):
        pltpu.make_async_copy(ys.at[z, e], yr.at[z, e], y_r.at[z, e]).start()

    settle(qb.at[1:nc], q_r.at[0])

    @pl.when(z > 0)
    def _():
        settle(qb.at[0], h_r)

    def query_chunk(j, carry):
        s0 = j * chunk
        for h in range(halves):
            for n in range(seqs):
                ext = qb[pl.ds(s0, chunk + 1), n, :, h * LANES:(h + 1) * LANES].astype(F32)
                value = feature(ext.reshape((chunk + 1) * rows, LANES), 0, h)
                value = value.astype(BF16).reshape(chunk // 2, 2, rows, LANES)
                for e in range(2):
                    qf[e, pl.ds(j * (chunk // 2), chunk // 2), n, :, h * LANES:(h + 1) * LANES] = value[:, e]
        return carry

    lax.fori_loop(0, chunks, query_chunk, 0)

    for h in range(halves):
        for e in range(2):
            for k in range(per_half):
                settle(yr.at[halves * k + parity[h], e], y_r.at[halves * k + parity[h], e])

            def gate_chunk(j, carry, h=h, e=e):
                s0 = j * chunk
                tiles = [yr[halves * k + parity[h], e, pl.ds(s0, chunk)].astype(F32).reshape(span, LANES)
                         for k in range(per_half)]
                for n in range(seqs):
                    filtered = jnp.concatenate([t[:, n * part:(n + 1) * part] for t in tiles], axis=1)
                    query = qf[e, pl.ds(s0, chunk), n, :, h * LANES:(h + 1) * LANES].astype(F32)
                    gated = query * filtered.reshape(chunk, rows, LANES)
                    gs[h, e, pl.ds(s0, chunk), n] = gated.astype(BF16)
                return carry

            lax.fori_loop(0, chunks // 2, gate_chunk, 0)

            def send_out(p, h=h, e=e):
                pltpu.make_async_remote_copy(
                    src_ref=gs.at[h, e, p // 2], dst_ref=out.at[:, :, half_cols(c, h)], send_sem=o_s,
                    recv_sem=o_r, device_id=(z, p), device_id_type=MESH).start()

            for dx in around:
                for dy in around:
                    p = across[dx] + along[dy] + e
                    if (dx, dy) != (0, 0):
                        send_out(p)
                    else:
                        @pl.when(p != c)
                        def _(p=p, send_out=send_out):
                            send_out(p)

                        @pl.when(p == c)
                        def _(h=h, e=e):
                            pltpu.make_async_copy(
                                gs.at[h, e, c // 2], out.at[:, :, half_cols(c, h)], o_r).start()

    settle(kv.at[:, :, 1:nc], kv_s)
    settle(qb.at[1:nc], q_s)
    settle(xs.at[1:nz, 0:pairs - 1, 0:LANES], x_s)
    settle(xs.at[1:nz, pairs - 1], x_s)
    settle(ys.at[1:nz], y_s)

    @pl.when(z < nz - 1)
    def _():
        settle(qb.at[nc], h_s)

    for h in range(halves):
        settle(gs.at[h, 0], o_s)
        settle(gs.at[h, 1, 1:nc // 2], o_s)
    settle(out, o_r)


def solution(mesh):
    nz, nc = mesh.shape["seq"], mesh.shape["ch"]

    def shards(proj, short_w, long_filter):
        seqs, rows, _, width = proj.shape
        chans = width // nc
        block = rows * nc
        halves = chans // LANES
        part = chans // nz
        pairs = seqs * part // LANES * (block // LANES)
        groups, length = long_filter.shape
        own = part // GSIZE
        by_component = jnp.transpose(proj, (0, 2, 1, 3))
        dma = pltpu.SemaphoreType.DMA
        sources = pltpu.VMEM((nz, pairs, LANES + rows, LANES), BF16)
        duo = seqs // pairs
        return pl.pallas_call(
            lambda *refs: kernel(nz, nc, *refs),
            out_shape=pltpu.VMEM((seqs, rows, width), BF16),
            in_specs=[pl.BlockSpec(memory_space=pltpu.HBM)] * 3,
            out_specs=pl.BlockSpec(memory_space=pl.ANY),
            scratch_shapes=[
                pltpu.VMEM((seqs, 3, rows, width), BF16),
                pltpu.VMEM(short_w.shape, F32),
                pltpu.VMEM(long_filter.shape, BF16),
                pltpu.VMEM((halves, pairs, nc + 1, duo, 2, rows, LANES), BF16),
                pltpu.VMEM((nc + 1, seqs, rows, chans), BF16),
                pltpu.VMEM((2, nc // 2, seqs, rows, chans), BF16),
                sources, sources,
                pltpu.VMEM((nz + 1, block, LANES), BF16),
                pltpu.VMEM((nz, rows, LANES), F32),
                pltpu.VMEM((short_w.shape[0], 2, rows, LANES), F32),
                pltpu.VMEM((nz, 2, nc // 2, rows, LANES), BF16),
                pltpu.VMEM((nz, 2, nc // 2, rows, LANES), BF16),
                pltpu.VMEM((halves, 2, nc // 2, seqs, rows, LANES), BF16),
                pltpu.VMEM((own, block, length), BF16),
                pltpu.VMEM((groups, length + LANES), F32),
                dma((3,)), dma, dma((halves, pairs)), dma, dma((2,)), dma, dma,
                dma, dma((nz, pairs)), dma, dma((nz, 2)), dma, dma,
            ],
            compiler_params=pltpu.CompilerParams(collective_id=0, has_side_effects=True),
            name="hyena",
        )(by_component, short_w, long_filter)

    in_specs = (P(None, ("seq", "ch"), None, None), P(None, None, "ch"), P("ch", None))
    out_specs = P(None, ("seq", "ch"), None)
    return jax.shard_map(shards, mesh=mesh, in_specs=in_specs, out_specs=out_specs, check_vma=False)
```

```python
import jax
import jax.numpy as jnp
from jax import lax
from jax.experimental import pallas as pl
from jax.experimental.pallas import tpu as pltpu
from jax.sharding import PartitionSpec as P

MESH = pl.DeviceIdType.MESH
GSIZE = 16
PIECES = 4
SHARES = 2
LANES = 128
F32 = jnp.float32
BF16 = jnp.bfloat16


def kernel(nz, nc, proj_in, w_in, lf_in, out, proj, w_ref, lf_ref, kv, qb, qf, xs, xr, xu, edge, wl, ys, yr, gs, toep, rev,
           in_r, kv_s, kv_r, q_s, q_r, h_s, h_r, x_s, x_r, y_s, y_r, o_s, o_r):
    z = lax.axis_index("seq")
    c = lax.axis_index("ch")
    seqs, _, rows, _ = proj.shape
    halves, pairs, chans = kv.shape[0], kv.shape[1], qb.shape[-1]
    duo = seqs // pairs
    block = rows * nc
    part = chans // nz
    per_half = LANES // part
    taps = w_ref.shape[0]
    chunk = 8
    chunks = nc // chunk
    span = chunk * rows
    folds = LANES // (duo * part)
    high = block // folds
    fold_slots = nc // folds
    strips = fold_slots // chunk
    own_half = lax.rem(z + c, halves)
    parity = [lax.rem(h + c, halves) for h in range(halves)]
    side = 4
    around = (2, 1, 3, 0)
    line = (4, 3, 5, 2, 6, 1, 7)

    def cols(p):
        return pl.ds(pl.multiple_of(p * chans, chans), chans)

    def half_cols(p, h):
        return pl.ds(pl.multiple_of(p * chans + h * LANES, LANES), LANES)

    def settle(ref, sem):
        pltpu.make_async_copy(ref, ref, sem).wait()

    across = [lax.rem(c // 8 + d, side) * 8 for d in range(side)]
    along = [lax.rem(c // 2 + d, side) * 2 for d in range(side)]
    core = [lax.rem(c + d, 2) for d in range(2)]

    def each_partner(body):
        for dx in around:
            for dy in around:
                for dc in (1, 0):
                    if (dx, dy, dc) != (0, 0, 0):
                        body(across[dx] + along[dy] + core[dc])

    barrier = pltpu.get_barrier_semaphore()

    def greet(p):
        pl.semaphore_signal(barrier, inc=1, device_id=(z, p), device_id_type=MESH)

    for n in range(seqs):
        pltpu.make_async_copy(proj_in.at[n], proj.at[n], in_r.at[0]).start()
    pltpu.make_async_copy(lf_in, lf_ref, in_r.at[1]).start()
    pltpu.make_async_copy(w_in, w_ref, in_r.at[2]).start()
    each_partner(greet)
    for d in line:
        pl.semaphore_signal(barrier, inc=1, device_id=(lax.rem(z + d, nz), c), device_id_type=MESH)
    settle(proj, in_r.at[0])
    last = c // (nc - 1)
    for h in range(halves):
        for a in range(pairs):
            pltpu.make_async_copy(
                proj.at[a * duo:(a + 1) * duo, 1:3, :, half_cols(c, h)], kv.at[h, a, c + 1],
                kv_r.at[h, a]).start()
    pltpu.make_async_copy(proj.at[:, 0, :, cols(c)], qb.at[c + 1], q_r.at[last]).start()
    pl.semaphore_wait(barrier, nc - 1 + nz - 1)

    for h in range(halves):
        for a in range(pairs):
            def send_kv(p, h=h, a=a):
                pltpu.make_async_remote_copy(
                    src_ref=proj.at[a * duo:(a + 1) * duo, 1:3, :, half_cols(p, h)],
                    dst_ref=kv.at[h, a, c + 1], send_sem=kv_s, recv_sem=kv_r.at[h, a],
                    device_id=(z, p), device_id_type=MESH).start()

            each_partner(send_kv)

    settle(lf_ref, in_r.at[1])
    settle(w_ref, in_r.at[2])

    length = lf_ref.shape[1]
    pieces = length // LANES
    flip = (lax.broadcasted_iota(jnp.int32, (LANES, LANES), 0)
            + lax.broadcasted_iota(jnp.int32, (LANES, LANES), 1)) == LANES - 1
    flip = flip.astype(F32).astype(BF16)
    rev[:, 0:LANES] = jnp.zeros((lf_ref.shape[0], LANES), F32)
    for m in range(pieces):
        rev[:, (m + 1) * LANES:(m + 2) * LANES] = jnp.dot(
            lf_ref[:, m * LANES:(m + 1) * LANES], flip, preferred_element_type=F32)
    groups = part // GSIZE
    own_row = (own_half * LANES + (z // halves) * part) // GSIZE
    for g in range(groups):
        for m in range(pieces):
            pair = rev[pl.ds(own_row + g, 1), m * LANES:(m + 2) * LANES]
            pair = jnp.broadcast_to(pair, (LANES, 2 * LANES))
            tile = pltpu.roll(pair, 1, 1, stride=1, stride_axis=0)[:, :LANES]
            tile = tile.astype(BF16)
            for th in range(2):
                for sh in range(2):
                    twice = m - th + sh
                    if twice % 2 == 0 and 0 <= twice // 2 < nz:
                        base = (twice // 2) * block + sh * LANES
                        toep[g, th * LANES:(th + 1) * LANES, base:base + LANES] = tile
        toep[g, 0:LANES, LANES:2 * LANES] = jnp.zeros((LANES, LANES), BF16)

    for k in range(taps):
        for i in range(2):
            mine = jnp.where(own_half == 0, w_ref[k, i + 1:i + 2, :LANES], w_ref[k, i + 1:i + 2, LANES:])
            mine = pltpu.roll(jnp.broadcast_to(mine, (rows, LANES)), LANES - (z // halves) * part, 1)
            wl[k, i] = jnp.concatenate([mine[:, :part]] * seqs, axis=1)

    xu[nz] = jnp.zeros(xu.shape[1:], BF16)
    row = lax.broadcasted_iota(jnp.int32, (rows, LANES), 0)
    for h in range(halves):
        for a in range(pairs):
            kv[h, a, 0] = jnp.zeros(kv.shape[3:], BF16)

    @pl.when(z == 0)
    def _():
        qb[0] = jnp.zeros(qb.shape[1:], BF16)

    def feature(ext, i, h):
        total = None
        for k in range(taps):
            term = w_ref[k, i:i + 1, h * LANES:(h + 1) * LANES] * ext[rows - k:rows - k + span]
            total = term if total is None else total + term
        return total

    def send_q(p):
        pltpu.make_async_remote_copy(
            src_ref=proj.at[:, 0, :, cols(p)], dst_ref=qb.at[c + 1], send_sem=q_s,
            recv_sem=q_r.at[last], device_id=(z, p), device_id_type=MESH).start()

    for h in range(halves):
        for a in range(pairs):
            settle(kv.at[h, a, 1:nc + 1], kv_r.at[h, a])

            def product_strip(k, carry, h=h, a=a):
                j = strips - 1 - k

                prods = []
                for f in range(folds):
                    for n in range(duo):
                        feats = []
                        for i in range(2):
                            ext = kv[h, a, pl.ds(f * fold_slots + j * chunk, chunk + 1), n, i].astype(F32)
                            feats.append(feature(ext.reshape((chunk + 1) * rows, LANES), i + 1, h))
                        prods.append(feats[0] * feats[1])
                t0 = pl.multiple_of(j * span, span)
                for k in range(per_half):
                    tile = jnp.concatenate([p[:, k * part:(k + 1) * part] for p in prods], axis=1)
                    xs[halves * k + parity[h], a, pl.ds(t0, span), :] = tile.astype(BF16)
                return carry

            lax.fori_loop(0, strips, product_strip, 0)

            tall = high
            if a == pairs - 1:
                tall = high + rows
                rims = []
                for n in range(seqs):
                    head, tail = kv.at[h, n // duo, 1, n % duo], kv.at[h, n // duo, nc, n % duo]
                    rim = pltpu.roll(head[1].astype(F32), 6, 0)
                    rim = jnp.where(row < 6, pltpu.roll(head[0].astype(F32), 4, 0), rim)
                    rim = jnp.where(row < 4, pltpu.roll(tail[1].astype(F32), 4, 0), rim)
                    rims.append(jnp.where(row < 2, pltpu.roll(tail[0].astype(F32), 2, 0), rim))
                for k in range(per_half):
                    tile = jnp.concatenate([r[:, k * part:(k + 1) * part] for r in rims], axis=1)
                    xs[halves * k + parity[h], a, high:high + rows, :] = tile.astype(BF16)

            for d in (2, 1, 3, 0):
                p = halves * lax.rem(z // halves + d, per_half) + parity[h]

                def send_x(p=p, a=a, tall=tall):
                    pltpu.make_async_remote_copy(
                        src_ref=xs.at[p, a, 0:tall], dst_ref=xr.at[z, a, 0:tall], send_sem=x_s, recv_sem=x_r.at[z, a],
                        device_id=(p, c), device_id_type=MESH).start()

                if d > 0:
                    send_x()
                else:
                    pl.when(own_half != h)(send_x)

            if (h, a) == (halves - 1, (pairs - 1) // 2):
                each_partner(send_q)

            @pl.when(own_half == h)
            def _():
                pltpu.make_async_copy(
                    xs.at[z, a, 0:tall], xr.at[z, a, 0:tall], x_r.at[z, a]).start()

    def pass_query_rim():
        settle(qb.at[nc], q_r.at[1])

        @pl.when(z < nz - 1)
        def _():
            pltpu.make_async_remote_copy(
                src_ref=qb.at[nc], dst_ref=qb.at[0], send_sem=h_s, recv_sem=h_r,
                device_id=(z + 1, c), device_id_type=MESH).start()

    pl.when(own_half != 0)(pass_query_rim)

    for s in range(nz):
        for a in range(pairs):
            settle(xr.at[s, a, 0:high + rows * (a // (pairs - 1))], x_r.at[s, a])
    for s in range(nz):
        tiles = [xr[s, a, :high, :] for a in range(pairs)]
        for f in range(folds):
            at = f * LANES // folds
            xu[nz - 1 - s, f * high:(f + 1) * high, :] = jnp.concatenate(
                [t[:, at:at + LANES // folds] for t in tiles], axis=1)
        edge[s] = xr[s, pairs - 1, high:high + rows, :].astype(F32)

    firsts, seconds = [], []
    for i in range(2):
        b2, b1 = edge[:, 2 * i, :], edge[:, 2 * i + 1, :]
        t0, t1 = edge[:, 4 + 2 * i, :], edge[:, 5 + 2 * i, :]
        block_row = lax.broadcasted_iota(jnp.int32, b2.shape, 0)
        b2 = jnp.where(block_row == 0, 0.0, pltpu.roll(b2, 1, 0))
        b1 = jnp.where(block_row == 0, 0.0, pltpu.roll(b1, 1, 0))
        w0, w1, w2 = wl[0, i], wl[1, i], wl[2, i]
        firsts.append(w0 * t0 + w1 * b1 + w2 * b2)
        seconds.append(w0 * t1 + w1 * t0 + w2 * b1)
    first, second = firsts[0] * firsts[1], seconds[0] * seconds[1]
    for s in range(1, nz):
        head = xu[nz - 1 - s, 0:2 * rows, :].astype(F32)
        at = lax.broadcasted_iota(jnp.int32, head.shape, 0)
        head = jnp.where(at == 0, first[s:s + 1], jnp.where(at == 1, second[s:s + 1], head))
        xu[nz - 1 - s, 0:2 * rows, :] = head.astype(BF16)

    lane = lax.broadcasted_iota(jnp.int32, (1, 2 * LANES), 1)

    def send_y(p, e):
        @pl.when(z != p)
        def _():
            pltpu.make_async_remote_copy(
                src_ref=ys.at[p, e], dst_ref=yr.at[z, e], send_sem=y_s, recv_sem=y_r.at[z, e],
                device_id=(p, c), device_id_type=MESH).start()

    for m in range(nz // 2):
        lags = 2 * m + 2
        even = xu[nz - 1 - 2 * m:nz - 1 - 2 * m + lags].reshape(lags * block, LANES)
        odd = xu[nz - 2 - 2 * m:nz - 2 - 2 * m + lags].reshape(lags * block, LANES)
        both = jnp.concatenate([even, odd], axis=1)
        total = None
        for g in range(groups):
            keep = ((lane // GSIZE) % groups == g).astype(F32).astype(BF16)
            term = jnp.dot(toep[g, :, 0:lags * block], both * keep, preferred_element_type=F32)
            total = term if total is None else total + term
        for i in range(2):
            result = total[:, i * LANES:(i + 1) * LANES].astype(BF16)
            result = result.reshape(nc // SHARES, SHARES, rows, LANES)
            for e in range(SHARES):
                ys[2 * m + i, e] = result[:, e]
        if m == nz // 2 - 1:
            pl.when(own_half == 0)(pass_query_rim)
        if m % 2 == 1:
            for p in range(2 * m - 2, 2 * m + 2):
                send_y(p, 0)
    for e in range(1, SHARES):
        for p in range(nz):
            send_y(p, e)
    for e in range(SHARES):
        pltpu.make_async_copy(ys.at[z, e], yr.at[z, e], y_r.at[z, e]).start()

    settle(qb.at[1:nc], q_r.at[0])

    @pl.when(z > 0)
    def _():
        settle(qb.at[0], h_r)

    def query_chunk(j, carry):
        s0 = j * chunk
        for h in range(halves):
            for n in range(seqs):
                ext = qb[pl.ds(s0, chunk + 1), n, :, h * LANES:(h + 1) * LANES].astype(F32)
                value = feature(ext.reshape((chunk + 1) * rows, LANES), 0, h)
                few = chunk // SHARES
                value = value.astype(BF16).reshape(few, SHARES, rows, LANES)
                for e in range(SHARES):
                    qf[e, pl.ds(j * few, few), n, :, h * LANES:(h + 1) * LANES] = value[:, e]
        return carry

    lax.fori_loop(0, chunks, query_chunk, 0)

    for h in range(halves):
        for e in range(SHARES):
            for k in range(per_half):
                settle(yr.at[halves * k + parity[h], e], y_r.at[halves * k + parity[h], e])

            def gate_chunk(j, carry, h=h, e=e):
                s0 = j * chunk
                tiles = [yr[halves * k + parity[h], e, pl.ds(s0, chunk)].astype(F32).reshape(span, LANES)
                         for k in range(per_half)]
                for n in range(seqs):
                    filtered = jnp.concatenate([t[:, n * part:(n + 1) * part] for t in tiles], axis=1)
                    query = qf[e, pl.ds(s0, chunk), n, :, h * LANES:(h + 1) * LANES].astype(F32)
                    gated = query * filtered.reshape(chunk, rows, LANES)
                    gs[h, e, pl.ds(s0, chunk), n] = gated.astype(BF16)
                return carry

            lax.fori_loop(0, chunks // SHARES, gate_chunk, 0)

            def send_out(p, h=h, e=e):
                pltpu.make_async_remote_copy(
                    src_ref=gs.at[h, e, p // SHARES], dst_ref=out.at[:, :, half_cols(c, h)], send_sem=o_s,
                    recv_sem=o_r, device_id=(z, p), device_id_type=MESH).start()

            for dx in around:
                for dy in around:
                    p = across[dx] + along[dy] + e
                    if (dx, dy) != (0, 0):
                        send_out(p)
                    else:
                        @pl.when(p != c)
                        def _(p=p, send_out=send_out):
                            send_out(p)

                        @pl.when(p == c)
                        def _(h=h, e=e):
                            pltpu.make_async_copy(
                                gs.at[h, e, c // SHARES], out.at[:, :, half_cols(c, h)], o_r).start()

    settle(kv.at[:, :, 1:nc], kv_s)
    settle(qb.at[1:nc], q_s)
    settle(xs.at[1:nz, 0:pairs - 1, 0:high], x_s)
    settle(xs.at[1:nz, pairs - 1], x_s)
    settle(ys.at[1:nz], y_s)

    @pl.when(z < nz - 1)
    def _():
        settle(qb.at[nc], h_s)

    settle(gs.at[:, 0:SHARES - 1], o_s)
    settle(gs.at[:, SHARES - 1, 1:nc // SHARES], o_s)
    settle(out, o_r)


def solution(mesh):
    nz, nc = mesh.shape["seq"], mesh.shape["ch"]

    def shards(proj, short_w, long_filter):
        seqs, rows, _, width = proj.shape
        chans = width // nc
        block = rows * nc
        halves = chans // LANES
        part = chans // nz
        pairs = PIECES
        groups, length = long_filter.shape
        own = part // GSIZE
        by_component = jnp.transpose(proj, (0, 2, 1, 3))
        dma = pltpu.SemaphoreType.DMA
        duo = seqs // PIECES
        sources = pltpu.VMEM((nz, PIECES, block * duo * part // LANES + rows, LANES), BF16)
        return pl.pallas_call(
            lambda *refs: kernel(nz, nc, *refs),
            out_shape=pltpu.VMEM((seqs, rows, width), BF16),
            in_specs=[pl.BlockSpec(memory_space=pltpu.HBM)] * 3,
            out_specs=pl.BlockSpec(memory_space=pl.ANY),
            scratch_shapes=[
                pltpu.VMEM((seqs, 3, rows, width), BF16),
                pltpu.VMEM(short_w.shape, F32),
                pltpu.VMEM(long_filter.shape, BF16),
                pltpu.VMEM((halves, pairs, nc + 1, duo, 2, rows, LANES), BF16),
                pltpu.VMEM((nc + 1, seqs, rows, chans), BF16),
                pltpu.VMEM((SHARES, nc // SHARES, seqs, rows, chans), BF16),
                sources, sources,
                pltpu.VMEM((nz + 1, block, LANES), BF16),
                pltpu.VMEM((nz, rows, LANES), F32),
                pltpu.VMEM((short_w.shape[0], 2, rows, LANES), F32),
                pltpu.VMEM((nz, SHARES, nc // SHARES, rows, LANES), BF16),
                pltpu.VMEM((nz, SHARES, nc // SHARES, rows, LANES), BF16),
                pltpu.VMEM((halves, SHARES, nc // SHARES, seqs, rows, LANES), BF16),
                pltpu.VMEM((own, block, length), BF16),
                pltpu.VMEM((groups, length + LANES), F32),
                dma((3,)), dma, dma((halves, pairs)), dma, dma((2,)), dma, dma,
                dma, dma((nz, pairs)), dma, dma((nz, SHARES)), dma, dma,
            ],
            compiler_params=pltpu.CompilerParams(collective_id=0, has_side_effects=True),
            name="hyena",
        )(by_component, short_w, long_filter)

    in_specs = (P(None, ("seq", "ch"), None, None), P(None, None, "ch"), P("ch", None))
    out_specs = P(None, ("seq", "ch"), None)
    return jax.shard_map(shards, mesh=mesh, in_specs=in_specs, out_specs=out_specs, check_vma=False)
```

```python
import jax
import jax.numpy as jnp
from jax import lax
from jax.experimental import pallas as pl
from jax.experimental.pallas import tpu as pltpu
from jax.sharding import PartitionSpec as P

MESH = pl.DeviceIdType.MESH
GSIZE = 16
PIECES = 4
SHARES = 2
LANES = 128
F32 = jnp.float32
BF16 = jnp.bfloat16


def kernel(nz, nc, proj_in, w_in, lf_in, out, proj, w_ref, lf_ref, kv, qb, qf, xs, xr, xu, edge, wl, ys, yr, gs, toep, rev,
           in_r, kv_s, kv_r, q_s, q_r, h_s, h_r, x_s, x_r, y_s, y_r, o_s, o_r):
    z = lax.axis_index("seq")
    c = lax.axis_index("ch")
    seqs, _, rows, _ = proj.shape
    halves, pairs, chans = kv.shape[0], kv.shape[1], qb.shape[-1]
    duo = seqs // pairs
    block = rows * nc
    part = chans // nz
    per_half = LANES // part
    taps = w_ref.shape[0]
    chunk = 8
    chunks = nc // chunk
    span = chunk * rows
    folds = LANES // (duo * part)
    high = block // folds
    fold_slots = nc // folds
    strips = fold_slots // chunk
    own_half = lax.rem(z + c, halves)
    parity = [lax.rem(h + c, halves) for h in range(halves)]
    side = 4
    around = (2, 1, 3, 0)
    line = (4, 3, 5, 2, 6, 1, 7)

    def cols(p):
        return pl.ds(pl.multiple_of(p * chans, chans), chans)

    def half_cols(p, h):
        return pl.ds(pl.multiple_of(p * chans + h * LANES, LANES), LANES)

    def settle(ref, sem):
        pltpu.make_async_copy(ref, ref, sem).wait()

    across = [lax.rem(c // 8 + d, side) * 8 for d in range(side)]
    along = [lax.rem(c // 2 + d, side) * 2 for d in range(side)]
    core = [lax.rem(c + d, 2) for d in range(2)]

    def each_partner(body):
        for dx in around:
            for dy in around:
                for dc in (1, 0):
                    if (dx, dy, dc) != (0, 0, 0):
                        body(across[dx] + along[dy] + core[dc])

    barrier = pltpu.get_barrier_semaphore()

    def greet(p):
        pl.semaphore_signal(barrier, inc=1, device_id=(z, p), device_id_type=MESH)

    each_partner(greet)
    for d in line:
        pl.semaphore_signal(barrier, inc=1, device_id=(lax.rem(z + d, nz), c), device_id_type=MESH)
    for n in range(seqs):
        pltpu.make_async_copy(proj_in.at[n], proj.at[n], in_r.at[n]).start()
    pltpu.make_async_copy(lf_in, lf_ref, in_r.at[seqs]).start()
    pltpu.make_async_copy(w_in, w_ref, in_r.at[seqs + 1]).start()
    last = c // (nc - 1)
    pl.semaphore_wait(barrier, nc - 1 + nz - 1)

    for h in range(halves):
        for a in range(pairs):
            if h == 0:
                for n in range(a * duo, (a + 1) * duo):
                    settle(proj.at[n], in_r.at[n])

            def send_kv(p, h=h, a=a):
                pltpu.make_async_remote_copy(
                    src_ref=proj.at[a * duo:(a + 1) * duo, 1:3, :, half_cols(p, h)],
                    dst_ref=kv.at[h, a, c + 1], send_sem=kv_s, recv_sem=kv_r.at[h, a],
                    device_id=(z, p), device_id_type=MESH).start()

            each_partner(send_kv)
            pltpu.make_async_copy(
                proj.at[a * duo:(a + 1) * duo, 1:3, :, half_cols(c, h)], kv.at[h, a, c + 1],
                kv_r.at[h, a]).start()
    pltpu.make_async_copy(proj.at[:, 0, :, cols(c)], qb.at[c + 1], q_r.at[last]).start()

    settle(lf_ref, in_r.at[seqs])
    settle(w_ref, in_r.at[seqs + 1])

    length = lf_ref.shape[1]
    pieces = length // LANES
    flip = (lax.broadcasted_iota(jnp.int32, (LANES, LANES), 0)
            + lax.broadcasted_iota(jnp.int32, (LANES, LANES), 1)) == LANES - 1
    flip = flip.astype(F32).astype(BF16)
    rev[:, 0:LANES] = jnp.zeros((lf_ref.shape[0], LANES), F32)
    for m in range(pieces):
        rev[:, (m + 1) * LANES:(m + 2) * LANES] = jnp.dot(
            lf_ref[:, m * LANES:(m + 1) * LANES], flip, preferred_element_type=F32)
    groups = part // GSIZE
    own_row = (own_half * LANES + (z // halves) * part) // GSIZE
    for g in range(groups):
        for m in range(pieces):
            pair = rev[pl.ds(own_row + g, 1), m * LANES:(m + 2) * LANES]
            pair = jnp.broadcast_to(pair, (LANES, 2 * LANES))
            tile = pltpu.roll(pair, 1, 1, stride=1, stride_axis=0)[:, :LANES]
            tile = tile.astype(BF16)
            for th in range(2):
                for sh in range(2):
                    twice = m - th + sh
                    if twice % 2 == 0 and 0 <= twice // 2 < nz:
                        base = (twice // 2) * block + sh * LANES
                        toep[g, th * LANES:(th + 1) * LANES, base:base + LANES] = tile
        toep[g, 0:LANES, LANES:2 * LANES] = jnp.zeros((LANES, LANES), BF16)

    for k in range(taps):
        for i in range(2):
            mine = jnp.where(own_half == 0, w_ref[k, i + 1:i + 2, :LANES], w_ref[k, i + 1:i + 2, LANES:])
            mine = pltpu.roll(jnp.broadcast_to(mine, (rows, LANES)), LANES - (z // halves) * part, 1)
            wl[k, i] = jnp.concatenate([mine[:, :part]] * seqs, axis=1)

    xu[nz] = jnp.zeros(xu.shape[1:], BF16)
    row = lax.broadcasted_iota(jnp.int32, (rows, LANES), 0)
    for h in range(halves):
        for a in range(pairs):
            kv[h, a, 0] = jnp.zeros(kv.shape[3:], BF16)

    @pl.when(z == 0)
    def _():
        qb[0] = jnp.zeros(qb.shape[1:], BF16)

    def feature(ext, i, h):
        total = None
        for k in range(taps):
            term = w_ref[k, i:i + 1, h * LANES:(h + 1) * LANES] * ext[rows - k:rows - k + span]
            total = term if total is None else total + term
        return total

    def send_q(p):
        pltpu.make_async_remote_copy(
            src_ref=proj.at[:, 0, :, cols(p)], dst_ref=qb.at[c + 1], send_sem=q_s,
            recv_sem=q_r.at[last], device_id=(z, p), device_id_type=MESH).start()

    for h in range(halves):
        for a in range(pairs):
            settle(kv.at[h, a, 1:nc + 1], kv_r.at[h, a])

            def product_strip(k, carry, h=h, a=a):
                j = strips - 1 - k

                prods = []
                for f in range(folds):
                    for n in range(duo):
                        feats = []
                        for i in range(2):
                            ext = kv[h, a, pl.ds(f * fold_slots + j * chunk, chunk + 1), n, i].astype(F32)
                            feats.append(feature(ext.reshape((chunk + 1) * rows, LANES), i + 1, h))
                        prods.append(feats[0] * feats[1])
                t0 = pl.multiple_of(j * span, span)
                for k in range(per_half):
                    tile = jnp.concatenate([p[:, k * part:(k + 1) * part] for p in prods], axis=1)
                    xs[halves * k + parity[h], a, pl.ds(t0, span), :] = tile.astype(BF16)
                return carry

            lax.fori_loop(0, strips, product_strip, 0)

            tall = high
            if a == pairs - 1:
                tall = high + rows
                rims = []
                for n in range(seqs):
                    head, tail = kv.at[h, n // duo, 1, n % duo], kv.at[h, n // duo, nc, n % duo]
                    rim = pltpu.roll(head[1].astype(F32), 6, 0)
                    rim = jnp.where(row < 6, pltpu.roll(head[0].astype(F32), 4, 0), rim)
                    rim = jnp.where(row < 4, pltpu.roll(tail[1].astype(F32), 4, 0), rim)
                    rims.append(jnp.where(row < 2, pltpu.roll(tail[0].astype(F32), 2, 0), rim))
                for k in range(per_half):
                    tile = jnp.concatenate([r[:, k * part:(k + 1) * part] for r in rims], axis=1)
                    xs[halves * k + parity[h], a, high:high + rows, :] = tile.astype(BF16)

            for d in (2, 1, 3, 0):
                p = halves * lax.rem(z // halves + d, per_half) + parity[h]

                def send_x(p=p, a=a, tall=tall):
                    pltpu.make_async_remote_copy(
                        src_ref=xs.at[p, a, 0:tall], dst_ref=xr.at[z, a, 0:tall], send_sem=x_s, recv_sem=x_r.at[z, a],
                        device_id=(p, c), device_id_type=MESH).start()

                if d > 0:
                    send_x()
                else:
                    pl.when(own_half != h)(send_x)

            if (h, a) == (halves - 1, (pairs - 1) // 2):
                each_partner(send_q)

            @pl.when(own_half == h)
            def _():
                pltpu.make_async_copy(
                    xs.at[z, a, 0:tall], xr.at[z, a, 0:tall], x_r.at[z, a]).start()

    def pass_query_rim():
        settle(qb.at[nc], q_r.at[1])

        @pl.when(z < nz - 1)
        def _():
            pltpu.make_async_remote_copy(
                src_ref=qb.at[nc], dst_ref=qb.at[0], send_sem=h_s, recv_sem=h_r,
                device_id=(z + 1, c), device_id_type=MESH).start()

    pl.when(own_half != 0)(pass_query_rim)

    for s in range(nz):
        for a in range(pairs):
            settle(xr.at[s, a, 0:high + rows * (a // (pairs - 1))], x_r.at[s, a])
    for s in range(nz):
        tiles = [xr[s, a, :high, :] for a in range(pairs)]
        for f in range(folds):
            at = f * LANES // folds
            xu[nz - 1 - s, f * high:(f + 1) * high, :] = jnp.concatenate(
                [t[:, at:at + LANES // folds] for t in tiles], axis=1)
        edge[s] = xr[s, pairs - 1, high:high + rows, :].astype(F32)

    firsts, seconds = [], []
    for i in range(2):
        b2, b1 = edge[:, 2 * i, :], edge[:, 2 * i + 1, :]
        t0, t1 = edge[:, 4 + 2 * i, :], edge[:, 5 + 2 * i, :]
        block_row = lax.broadcasted_iota(jnp.int32, b2.shape, 0)
        b2 = jnp.where(block_row == 0, 0.0, pltpu.roll(b2, 1, 0))
        b1 = jnp.where(block_row == 0, 0.0, pltpu.roll(b1, 1, 0))
        w0, w1, w2 = wl[0, i], wl[1, i], wl[2, i]
        firsts.append(w0 * t0 + w1 * b1 + w2 * b2)
        seconds.append(w0 * t1 + w1 * t0 + w2 * b1)
    first, second = firsts[0] * firsts[1], seconds[0] * seconds[1]
    for s in range(1, nz):
        head = xu[nz - 1 - s, 0:2 * rows, :].astype(F32)
        at = lax.broadcasted_iota(jnp.int32, head.shape, 0)
        head = jnp.where(at == 0, first[s:s + 1], jnp.where(at == 1, second[s:s + 1], head))
        xu[nz - 1 - s, 0:2 * rows, :] = head.astype(BF16)

    lane = lax.broadcasted_iota(jnp.int32, (1, 2 * LANES), 1)

    for m in range(nz // 2):
        lags = 2 * m + 2
        even = xu[nz - 1 - 2 * m:nz - 1 - 2 * m + lags].reshape(lags * block, LANES)
        odd = xu[nz - 2 - 2 * m:nz - 2 - 2 * m + lags].reshape(lags * block, LANES)
        both = jnp.concatenate([even, odd], axis=1)
        total = None
        for g in range(groups):
            keep = ((lane // GSIZE) % groups == g).astype(F32).astype(BF16)
            term = jnp.dot(toep[g, :, 0:lags * block], both * keep, preferred_element_type=F32)
            total = term if total is None else total + term
        for i in range(2):
            result = total[:, i * LANES:(i + 1) * LANES].astype(BF16)
            result = result.reshape(nc // SHARES, SHARES, rows, LANES)
            for e in range(SHARES):
                ys[2 * m + i, e] = result[:, e]
    for e in range(SHARES):
        for p in (0, 4, 1, 5, 2, 6, 3, 7):
            @pl.when(z != p)
            def _(p=p, e=e):
                pltpu.make_async_remote_copy(
                    src_ref=ys.at[p, e], dst_ref=yr.at[z, e], send_sem=y_s, recv_sem=y_r.at[z, e],
                    device_id=(p, c), device_id_type=MESH).start()

        if e == 0:
            pl.when(own_half == 0)(pass_query_rim)
        pltpu.make_async_copy(ys.at[z, e], yr.at[z, e], y_r.at[z, e]).start()

    settle(qb.at[1:nc], q_r.at[0])

    @pl.when(z > 0)
    def _():
        settle(qb.at[0], h_r)

    def query_chunk(j, carry):
        s0 = j * chunk
        for h in range(halves):
            for n in range(seqs):
                ext = qb[pl.ds(s0, chunk + 1), n, :, h * LANES:(h + 1) * LANES].astype(F32)
                value = feature(ext.reshape((chunk + 1) * rows, LANES), 0, h)
                few = chunk // SHARES
                value = value.astype(BF16).reshape(few, SHARES, rows, LANES)
                for e in range(SHARES):
                    qf[e, pl.ds(j * few, few), n, :, h * LANES:(h + 1) * LANES] = value[:, e]
        return carry

    lax.fori_loop(0, chunks, query_chunk, 0)

    for h in range(halves):
        for e in range(SHARES):
            for k in range(per_half):
                settle(yr.at[halves * k + parity[h], e], y_r.at[halves * k + parity[h], e])

            def gate_chunk(j, carry, h=h, e=e):
                s0 = j * chunk
                tiles = [yr[halves * k + parity[h], e, pl.ds(s0, chunk)].astype(F32).reshape(span, LANES)
                         for k in range(per_half)]
                for n in range(seqs):
                    filtered = jnp.concatenate([t[:, n * part:(n + 1) * part] for t in tiles], axis=1)
                    query = qf[e, pl.ds(s0, chunk), n, :, h * LANES:(h + 1) * LANES].astype(F32)
                    gated = query * filtered.reshape(chunk, rows, LANES)
                    gs[h, e, pl.ds(s0, chunk), n] = gated.astype(BF16)
                return carry

            lax.fori_loop(0, chunks // SHARES, gate_chunk, 0)

            def send_out(p, h=h, e=e):
                pltpu.make_async_remote_copy(
                    src_ref=gs.at[h, e, p // SHARES], dst_ref=out.at[:, :, half_cols(c, h)], send_sem=o_s,
                    recv_sem=o_r, device_id=(z, p), device_id_type=MESH).start()

            for dx in around:
                for dy in around:
                    p = across[dx] + along[dy] + e
                    if (dx, dy) != (0, 0):
                        send_out(p)
                    else:
                        @pl.when(p != c)
                        def _(p=p, send_out=send_out):
                            send_out(p)

                        @pl.when(p == c)
                        def _(h=h, e=e):
                            pltpu.make_async_copy(
                                gs.at[h, e, c // SHARES], out.at[:, :, half_cols(c, h)], o_r).start()

    settle(kv.at[:, :, 1:nc], kv_s)
    settle(qb.at[1:nc], q_s)
    settle(xs.at[1:nz, 0:pairs - 1, 0:high], x_s)
    settle(xs.at[1:nz, pairs - 1], x_s)
    settle(ys.at[1:nz], y_s)

    @pl.when(z < nz - 1)
    def _():
        settle(qb.at[nc], h_s)

    settle(gs.at[:, 0:SHARES - 1], o_s)
    settle(gs.at[:, SHARES - 1, 1:nc // SHARES], o_s)
    settle(out, o_r)


def solution(mesh):
    nz, nc = mesh.shape["seq"], mesh.shape["ch"]

    def shards(proj, short_w, long_filter):
        seqs, rows, _, width = proj.shape
        chans = width // nc
        block = rows * nc
        halves = chans // LANES
        part = chans // nz
        pairs = PIECES
        groups, length = long_filter.shape
        own = part // GSIZE
        by_component = jnp.transpose(proj, (0, 2, 1, 3))
        dma = pltpu.SemaphoreType.DMA
        duo = seqs // PIECES
        sources = pltpu.VMEM((nz, PIECES, block * duo * part // LANES + rows, LANES), BF16)
        return pl.pallas_call(
            lambda *refs: kernel(nz, nc, *refs),
            out_shape=pltpu.VMEM((seqs, rows, width), BF16),
            in_specs=[pl.BlockSpec(memory_space=pltpu.HBM)] * 3,
            out_specs=pl.BlockSpec(memory_space=pl.ANY),
            scratch_shapes=[
                pltpu.VMEM((seqs, 3, rows, width), BF16),
                pltpu.VMEM(short_w.shape, F32),
                pltpu.VMEM(long_filter.shape, BF16),
                pltpu.VMEM((halves, pairs, nc + 1, duo, 2, rows, LANES), BF16),
                pltpu.VMEM((nc + 1, seqs, rows, chans), BF16),
                pltpu.VMEM((SHARES, nc // SHARES, seqs, rows, chans), BF16),
                sources, sources,
                pltpu.VMEM((nz + 1, block, LANES), BF16),
                pltpu.VMEM((nz, rows, LANES), F32),
                pltpu.VMEM((short_w.shape[0], 2, rows, LANES), F32),
                pltpu.VMEM((nz, SHARES, nc // SHARES, rows, LANES), BF16),
                pltpu.VMEM((nz, SHARES, nc // SHARES, rows, LANES), BF16),
                pltpu.VMEM((halves, SHARES, nc // SHARES, seqs, rows, LANES), BF16),
                pltpu.VMEM((own, block, length), BF16),
                pltpu.VMEM((groups, length + LANES), F32),
                dma((seqs + 2,)), dma, dma((halves, pairs)), dma, dma((2,)), dma, dma,
                dma, dma((nz, pairs)), dma, dma((nz, SHARES)), dma, dma,
            ],
            compiler_params=pltpu.CompilerParams(collective_id=0, has_side_effects=True),
            name="hyena",
        )(by_component, short_w, long_filter)

    in_specs = (P(None, ("seq", "ch"), None, None), P(None, None, "ch"), P("ch", None))
    out_specs = P(None, ("seq", "ch"), None)
    return jax.shard_map(shards, mesh=mesh, in_specs=in_specs, out_specs=out_specs, check_vma=False)
```
